32 devices in a mesh: dp: 8 (over z, core), tensor: 4 (over y, x).
Axes of the slice: x: 2, y: 2, z: 4, core: 2. Of those that a mesh axis runs over, the one named last changes fastest.
Arguments:
- block_input: bfloat16 [8192, 2048], P('dp'), may hold values from -6 to 6
- block_owner: int32 [64], P('dp'), may hold values from 0 to 63, as said below
- token_mask: int32 [8192], P('dp'), may hold values from 0 to 1, as said below
- attention_gain: float32 [2048], replicated, may hold values from 0.5 to 1.5
- query_weight: bfloat16 [2048, 2048], P(None, 'tensor')
- key_weight: bfloat16 [2048, 2048], P(None, 'tensor')
- value_weight: bfloat16 [2048, 2048], P(None, 'tensor'), may hold values from -0.125 to 0.125
- output_weight: bfloat16 [2048, 2048], P('tensor'), may hold values from -0.5 to 0.5
- feedforward_gain: float32 [2048], replicated, may hold values from 0.5 to 1.5
- gate_weight: bfloat16 [2048, 8192], P(None, 'tensor'), may hold values from -0.125 to 0.125
- up_weight: bfloat16 [2048, 8192], P(None, 'tensor'), may hold values from -0.125 to 0.125
- down_weight: bfloat16 [8192, 2048], P('tensor'), may hold values from -0.0625 to 0.0625
- cotangent: bfloat16 [8192, 2048], P('dp'), may hold values from -6 to 6
Outputs:
- block_output: bfloat16 [8192, 2048], P('dp')
- input_gradient: float32 [8192, 2048], P('dp')
- attention_gain_gradient: float32 [2048], P('dp')
- query_gradient: float32 [2048, 2048], P('dp', 'tensor')
- key_gradient: float32 [2048, 2048], P('dp', 'tensor')
- value_gradient: float32 [2048, 2048], P('dp', 'tensor')
- output_gradient: float32 [2048, 2048], P('tensor', 'dp')
- feedforward_gain_gradient: float32 [2048], P('dp')
- gate_gradient: float32 [2048, 8192], P('dp', 'tensor')
- up_gradient: float32 [2048, 8192], P('dp', 'tensor')
- down_gradient: float32 [8192, 2048], P('tensor', 'dp')
The draws below stay inside these ranges and needn't reach their ends.
Inputs may be any that keep to these rules, and one draw needn't show every extreme that they name: `block_owner`: each sequence takes one to 4 consecutive blocks of a single index of dp; a block's entry is the index of its sequence's first block in the whole array. The first 4 blocks of every index of dp form one sequence. `token_mask`: in each sequence the real tokens come first and there is at least one unless the sequence is a single block of padding; the first sequence of every index of dp is all real (512 tokens). Blocks after the last real token of an index of dp are padding, each its own sequence.
All inputs are finite; a program needn't handle non-finite values.
Results may differ from the reference program's by a relative error of at most 0.014.
Values sent between devices are 32-bit elements; how exact they have to be, the bound alone decides.
No kernel may reach another device: no remote copies, remote signals or barrier semaphores. Data moves between devices by JAX's collectives and lax.ppermute only.
A program may use at most 384 MiB of HBM per device.

```python
import jax
import jax.numpy as jnp
from jax import lax

D = 2048
HEADS = 32
HD = 64
FF = 8192
TOK_DEV = 1024
BLK = 128
SEQ_BLOCKS = 4
GROUP = 512
WINDOW = 896
TOKENS = 8192


def layout_tables(key):
    device_count = TOKENS // TOK_DEV
    per_device = TOK_DEV // BLK
    start_bits = jax.random.randint(jax.random.fold_in(key, 101), (device_count, per_device), 0, 2)
    live_blocks = jax.random.randint(jax.random.fold_in(key, 102), (device_count,), SEQ_BLOCKS, per_device + 1)
    tail_rows = jax.random.randint(jax.random.fold_in(key, 103), (device_count, per_device), 1, BLK + 1)
    block_index = jnp.arange(per_device, dtype=jnp.int32)

    def advance(carry, column):
        first_seen, run_length = carry
        index, bits = column
        fresh = (index == 0) | (index == SEQ_BLOCKS) | (index >= live_blocks) | (index > SEQ_BLOCKS) & ((bits > 0) | (run_length >= SEQ_BLOCKS))
        first_seen = jnp.where(fresh, index, first_seen)
        run_length = jnp.where(fresh, jnp.ones_like(run_length), run_length + 1)
        return ((first_seen, run_length), (first_seen, fresh))
    start_state = (jnp.zeros((device_count,), jnp.int32), jnp.zeros((device_count,), jnp.int32))
    _, (firsts, starts) = lax.scan(advance, start_state, (block_index, start_bits.T))
    firsts = firsts.T
    starts = starts.T
    next_start = jnp.concatenate([starts[:, 1:], jnp.ones((device_count, 1), dtype=bool)], axis=1)
    alive = block_index[None, :] < live_blocks[:, None]
    ending = next_start & (block_index[None, :] >= SEQ_BLOCKS)
    filled = jnp.where(alive, jnp.where(ending, tail_rows, BLK), 0)
    owners = firsts + jnp.arange(device_count, dtype=jnp.int32)[:, None] * per_device
    row_in_block = jnp.arange(BLK, dtype=jnp.int32)
    token_bits = (row_in_block[None, None, :] < filled[:, :, None]).astype(jnp.int32)
    return (owners.reshape(-1).astype(jnp.int32), token_bits.reshape(-1))


def paired_weights(key):
    width = HEADS * HD
    base = jax.random.normal(jax.random.fold_in(key, 201), (D, width), jnp.float32) * D ** (-0.5)
    other = jax.random.normal(jax.random.fold_in(key, 202), (D, width), jnp.float32) * D ** (-0.5)
    return (base, other)


def draw_block_owner(key, part):
    return layout_tables(key)[0]


def draw_token_mask(key, part):
    return layout_tables(key)[1]


def draw_query_weight(key, part):
    return paired_weights(key)[0].astype(jnp.bfloat16)


def draw_key_weight(key, part):
    return paired_weights(key)[1].astype(jnp.bfloat16)


def strengthened(drawn, own_key, source, target, blocks, factor):
    def block_of(position):
        return (jnp.arange(drawn.shape[position]) // (drawn.shape[position] // blocks)).reshape((-1,) + (1,) * (drawn.ndim - 1 - position))

    near = jax.random.permutation(own_key, blocks)[block_of(target)]
    other_side = (block_of(target) + blocks // 2) % blocks
    return jnp.where((block_of(source) == near) | (block_of(source) == other_side), factor * drawn, drawn)


def shard_levels(key, extent, shards, low, top_value):
    level = 1.0
    for position, parts in shards:
        steps = jax.random.uniform(jax.random.fold_in(jax.random.fold_in(key, 6), position), (parts,), jnp.float32, low / len(shards), top_value / len(shards))
        level = level * jnp.repeat(jnp.exp(steps), extent[position] // parts).reshape((-1,) + (1,) * (len(extent) - 1 - position))
    return level


def bell_draw(own_key, shape, scale, limit, split=(), held_as=jnp.bfloat16):
    values = jax.random.normal(own_key, shape, jnp.float32) * scale
    if len(split) > 0:
        values = shard_levels(own_key, shape, split, -0.22, 0.18) * values
    return jnp.clip(values, min=-limit, max=limit).astype(held_as)


def heavy_noise(rng, dims, spread, most, shards, heavy, kind=jnp.bfloat16):
    entries = spread * jax.random.normal(rng, dims, jnp.float32)
    if shards:
        entries = entries * shard_levels(rng, dims, shards, -0.22, 0.18)
    return jnp.clip(strengthened(entries, jax.random.fold_in(rng, 3), *heavy), -most, most).astype(kind)


def setup_inputs(seed: int = 0) -> dict:
    arg_keys = jax.random.split(jax.random.key(seed), 14)
    return {
        "block_input": heavy_noise(arg_keys[0], (TOKENS, D), 1.0, 6.0, ((0, 8),), (0, 1, 8, 2.0)),
        "block_owner": draw_block_owner(jax.random.fold_in(arg_keys[13], 71), 0),
        "token_mask": draw_token_mask(jax.random.fold_in(arg_keys[13], 71), 0),
        "attention_gain": jnp.clip(1.0 + 0.1 * jax.random.normal(arg_keys[3], (D,), jnp.float32), 0.5, 1.5),
        "query_weight": draw_query_weight(jax.random.fold_in(arg_keys[13], 71), 0),
        "key_weight": draw_key_weight(jax.random.fold_in(arg_keys[13], 71), 0),
        "value_weight": bell_draw(arg_keys[6], (D, HEADS * HD), D ** -0.5, 0.125, ((1, 4),)),
        "output_weight": bell_draw(arg_keys[7], (HEADS * HD, D), (HEADS * HD // 16) ** -0.5, 0.5, ((0, 4),)),
        "feedforward_gain": jnp.clip(1.0 + 0.1 * jax.random.normal(arg_keys[8], (D,), jnp.float32), 0.5, 1.5),
        "gate_weight": bell_draw(arg_keys[9], (D, FF), D ** -0.5, 0.125, ((1, 4),)),
        "up_weight": bell_draw(arg_keys[10], (D, FF), D ** -0.5, 0.125, ((1, 4),)),
        "down_weight": bell_draw(arg_keys[11], (FF, D), FF ** -0.5, 0.0625, ((0, 4),)),
        "cotangent": heavy_noise(arg_keys[12], (TOKENS, D), 1.0, 6.0, ((0, 8),), (0, 1, 8, 2.0)),
    }


NORM_EPS = 1e-05
ROPE_BASE = 130000.0
MASKED = -1e+30

def rms_forward(values, norm_gain):
    inverse = lax.rsqrt(lax.optimization_barrier(jnp.mean(values * values, axis=-1, keepdims=True)) + NORM_EPS)
    return (values * inverse * norm_gain, inverse)

def rms_backward(values, inverse, norm_gain, upstream):
    unit_rows = values * inverse
    gain_part = lax.optimization_barrier(jnp.sum(upstream * unit_rows, axis=0))
    scaled = upstream * norm_gain
    back = inverse * (scaled - unit_rows * lax.optimization_barrier(jnp.mean(scaled * unit_rows, axis=-1, keepdims=True)))
    return (back, gain_part)

def rope_tables(positions, width):
    half_width = width // 2
    frequency = ROPE_BASE ** (-(jnp.arange(half_width, dtype=jnp.float32) * 2.0 / width))
    angles = positions.astype(jnp.float32)[:, None] * frequency[None, :]
    return (jnp.cos(angles)[:, None, :], jnp.sin(angles)[:, None, :])

def rotate(values, cosine, sine):
    half_width = values.shape[-1] // 2
    first_half = values[..., :half_width]
    second_half = values[..., half_width:]
    return jnp.concatenate([first_half * cosine - second_half * sine, second_half * cosine + first_half * sine], axis=-1)

def allowed_keys(query_owner, query_pos, key_owner, key_pos, key_valid):
    same = query_owner[:, None] == key_owner[None, :]
    causal = key_pos[None, :] <= query_pos[:, None]
    usable = (key_valid[None, :] > 0) | (key_pos[None, :] == 0)
    return same & causal & usable

def masked_scores(query_block, key_block, allowed, scale):
    scores = jnp.einsum('qhd,khd->hqk', query_block.astype(jnp.float32), key_block.astype(jnp.float32)) * scale
    return jnp.where(allowed[None], scores, MASKED)

def reference(block_input, block_owner, token_mask, attention_gain, query_weight, key_weight, value_weight, output_weight, feedforward_gain, gate_weight, up_weight, down_weight, cotangent):
    row_count = block_input.shape[0]
    scale = HD ** (-0.5)
    front = WINDOW - GROUP
    owners = jnp.repeat(block_owner, BLK, total_repeat_length=row_count)
    row_index = jnp.arange(row_count, dtype=jnp.int32)
    positions = ((row_index // BLK - owners) * BLK + row_index % BLK).astype(jnp.int32)
    cosine, sine = rope_tables(positions, HD)
    key_owner = jnp.concatenate([jnp.full((front,), -1, jnp.int32), owners.astype(jnp.int32)])
    key_pos = jnp.concatenate([jnp.zeros((front,), jnp.int32), positions])
    key_valid = jnp.concatenate([jnp.zeros((front,), jnp.int32), token_mask.astype(jnp.int32)])
    inputs_f = block_input.astype(jnp.float32)
    normed_one, inverse_one = rms_forward(inputs_f, attention_gain)
    act_one = normed_one.astype(jnp.bfloat16)

    def project(weight):
        return jnp.dot(act_one, weight, preferred_element_type=jnp.float32).reshape(row_count, HEADS, HD)
    queries = rotate(project(query_weight), cosine, sine).astype(jnp.bfloat16)
    keys_rot = rotate(project(key_weight), cosine, sine).astype(jnp.bfloat16)
    values_b = project(value_weight).astype(jnp.bfloat16)
    pad_block = jnp.zeros((front, HEADS, HD), jnp.bfloat16)
    key_pad = jnp.concatenate([pad_block, keys_rot], axis=0)
    value_pad = jnp.concatenate([pad_block, values_b], axis=0)
    group_ids = jnp.arange(row_count // GROUP, dtype=jnp.int32)

    def group_mask(start):
        return allowed_keys(lax.dynamic_slice_in_dim(owners, start, GROUP), lax.dynamic_slice_in_dim(positions, start, GROUP), lax.dynamic_slice_in_dim(key_owner, start, WINDOW), lax.dynamic_slice_in_dim(key_pos, start, WINDOW), lax.dynamic_slice_in_dim(key_valid, start, WINDOW))

    def forward_group(carry, group):
        start = group * GROUP
        scores = masked_scores(lax.dynamic_slice_in_dim(queries, start, GROUP), lax.dynamic_slice_in_dim(key_pad, start, WINDOW), group_mask(start), scale)
        peak = lax.optimization_barrier(jnp.max(scores, axis=-1, keepdims=True))
        logsum = peak + jnp.log(lax.optimization_barrier(jnp.sum(jnp.exp(scores - peak), axis=-1, keepdims=True)))
        probs = jnp.exp(scores - logsum).astype(jnp.bfloat16)
        result = jnp.einsum('hqk,khd->qhd', probs.astype(jnp.float32), lax.dynamic_slice_in_dim(value_pad, start, WINDOW).astype(jnp.float32))
        return (carry, (result.astype(jnp.bfloat16), logsum))
    _, (attn_groups, logsums) = lax.scan(forward_group, jnp.int32(0), group_ids)
    attn_heads = attn_groups.reshape(row_count, HEADS, HD)
    attn_flat = attn_heads.reshape(row_count, HEADS * HD)
    hidden_sum = inputs_f + jnp.dot(attn_flat, output_weight, preferred_element_type=jnp.float32)
    normed_two, inverse_two = rms_forward(hidden_sum, feedforward_gain)
    act_two = normed_two.astype(jnp.bfloat16)
    gate_pre = jnp.dot(act_two, gate_weight, preferred_element_type=jnp.float32)
    up_pre = jnp.dot(act_two, up_weight, preferred_element_type=jnp.float32)
    sigmoid_gate = jax.nn.sigmoid(gate_pre)
    inner = (gate_pre * sigmoid_gate * up_pre).astype(jnp.bfloat16)
    block_output = (hidden_sum + jnp.dot(inner, down_weight, preferred_element_type=jnp.float32)).astype(jnp.bfloat16)
    grad_rows = jnp.where(token_mask[:, None] > 0, cotangent, jnp.zeros_like(cotangent))
    down_gradient = jnp.dot(inner.T, grad_rows, preferred_element_type=jnp.float32)
    inner_grad = jnp.dot(grad_rows, down_weight.T, preferred_element_type=jnp.float32)
    gate_back = (inner_grad * up_pre * sigmoid_gate * (1.0 + gate_pre * (1.0 - sigmoid_gate))).astype(jnp.bfloat16)
    up_back = (inner_grad * gate_pre * sigmoid_gate).astype(jnp.bfloat16)
    gate_gradient = jnp.dot(act_two.T, gate_back, preferred_element_type=jnp.float32)
    up_gradient = jnp.dot(act_two.T, up_back, preferred_element_type=jnp.float32)
    act_two_grad = jnp.dot(gate_back, gate_weight.T, preferred_element_type=jnp.float32) + jnp.dot(up_back, up_weight.T, preferred_element_type=jnp.float32)
    hidden_norm_back, feedforward_gain_gradient = rms_backward(hidden_sum, inverse_two, feedforward_gain, act_two_grad)
    hidden_grad = grad_rows.astype(jnp.float32) + hidden_norm_back
    hidden_back = hidden_grad.astype(jnp.bfloat16)
    output_gradient = jnp.dot(attn_flat.T, hidden_back, preferred_element_type=jnp.float32)
    attention_grad = jnp.dot(hidden_back, output_weight.T, preferred_element_type=jnp.float32).astype(jnp.bfloat16).reshape(row_count, HEADS, HD)

    def backward_group(carry, inputs):
        key_acc, value_acc = carry
        group, logsum = inputs
        start = group * GROUP
        query_block = lax.dynamic_slice_in_dim(queries, start, GROUP).astype(jnp.float32)
        key_block = lax.dynamic_slice_in_dim(key_pad, start, WINDOW).astype(jnp.float32)
        value_block = lax.dynamic_slice_in_dim(value_pad, start, WINDOW).astype(jnp.float32)
        grad_block = lax.dynamic_slice_in_dim(attention_grad, start, GROUP).astype(jnp.float32)
        attn_block = lax.dynamic_slice_in_dim(attn_heads, start, GROUP).astype(jnp.float32)
        scores = masked_scores(query_block, key_block, group_mask(start), scale)
        probs_f = jnp.exp(scores - logsum)
        probs_b = probs_f.astype(jnp.bfloat16).astype(jnp.float32)
        value_part = jnp.einsum('hqk,qhd->khd', probs_b, grad_block)
        prob_grad = jnp.einsum('qhd,khd->hqk', grad_block, value_block)
        delta = lax.optimization_barrier(jnp.sum(grad_block * attn_block, axis=-1)).T[:, :, None]
        score_grad = (probs_f * (prob_grad - delta) * scale).astype(jnp.bfloat16).astype(jnp.float32)
        query_part = jnp.einsum('hqk,khd->qhd', score_grad, key_block)
        key_part = jnp.einsum('hqk,qhd->khd', score_grad, query_block)
        key_acc = lax.dynamic_update_slice_in_dim(key_acc, lax.dynamic_slice_in_dim(key_acc, start, WINDOW) + key_part, start, 0)
        value_acc = lax.dynamic_update_slice_in_dim(value_acc, lax.dynamic_slice_in_dim(value_acc, start, WINDOW) + value_part, start, 0)
        return ((key_acc, value_acc), query_part)
    zeros_acc = jnp.zeros((front + row_count, HEADS, HD), jnp.float32)
    (key_acc, value_acc), query_parts = lax.scan(backward_group, (zeros_acc, zeros_acc), (group_ids, logsums))
    query_back = rotate(query_parts.reshape(row_count, HEADS, HD), cosine, -sine).astype(jnp.bfloat16).reshape(row_count, HEADS * HD)
    key_back = rotate(key_acc[front:], cosine, -sine).astype(jnp.bfloat16).reshape(row_count, HEADS * HD)
    value_back = value_acc[front:].astype(jnp.bfloat16).reshape(row_count, HEADS * HD)
    query_gradient = jnp.dot(act_one.T, query_back, preferred_element_type=jnp.float32)
    key_gradient = jnp.dot(act_one.T, key_back, preferred_element_type=jnp.float32)
    value_gradient = jnp.dot(act_one.T, value_back, preferred_element_type=jnp.float32)
    act_one_grad = jnp.dot(query_back, query_weight.T, preferred_element_type=jnp.float32) + jnp.dot(key_back, key_weight.T, preferred_element_type=jnp.float32) + jnp.dot(value_back, value_weight.T, preferred_element_type=jnp.float32)
    input_norm_back, attention_gain_gradient = rms_backward(inputs_f, inverse_one, attention_gain, act_one_grad)
    input_gradient = hidden_grad + input_norm_back
    return (block_output, input_gradient, attention_gain_gradient, query_gradient, key_gradient, value_gradient, output_gradient, feedforward_gain_gradient, gate_gradient, up_gradient, down_gradient)
```

```python
import functools

import jax
import jax.numpy as jnp
from jax import lax
from jax.experimental import pallas as pl
from jax.experimental.pallas import tpu as pltpu
from jax.sharding import PartitionSpec as P


HD = 64
BLK = 128
SEQ_BLOCKS = 4
FIRST = BLK * SEQ_BLOCKS

NORM_EPS = 1e-05
ROPE_BASE = 130000.0
MASKED = -1e30


F32 = jnp.float32
BF16 = jnp.bfloat16


def mm(a, b):
    return jnp.dot(a, b, preferred_element_type=F32)


def mm_nt(a, b):
    return lax.dot_general(a, b, (((1,), (1,)), ((), ())), preferred_element_type=F32)


def mm_tn(a, b):
    return lax.dot_general(a, b, (((0,), (0,)), ((), ())), preferred_element_type=F32)


def rope_tables(positions, width, lanes):
    half_width = width // 2
    frequency = ROPE_BASE ** (-(jnp.arange(half_width, dtype=F32) * 2.0 / width))
    angles = positions.astype(F32)[:, None] * frequency[None, :]
    cosine, sine = jnp.cos(angles), jnp.sin(angles)
    copies = lanes // width
    return (
        jnp.concatenate([cosine, cosine] * copies, axis=1),
        jnp.concatenate([-sine, sine] * copies, axis=1),
    )


def turn(values, cosine, signed_sine):
    lanes = values.shape[1]
    half = HD // 2
    lane = lax.broadcasted_iota(jnp.int32, values.shape, 1)
    other = jnp.where(
        lane % HD < half,
        pltpu.roll(values, lanes - half, 1),
        pltpu.roll(values, half, 1),
    )
    return values * cosine + other * signed_sine


def head_probs(q, k, mask):
    scores = mm_nt(q, k) * HD ** (-0.5)
    scores = jnp.where(mask > 0, scores, MASKED)
    peak = jnp.max(scores, axis=-1, keepdims=True)
    raised = jnp.exp(scores - peak)
    return raised * (1.0 / jnp.sum(raised, axis=-1, keepdims=True))


def attend_body(act, wq, wk, wv, cos, sin, mask, q_out, k_out, v_out, attn_out):
    rows = act[...]
    q = turn(mm(rows, wq[...]), cos[...], sin[...]).astype(BF16)
    k = turn(mm(rows, wk[...]), cos[...], sin[...]).astype(BF16)
    v = mm(rows, wv[...]).astype(BF16)
    q_out[...] = q
    k_out[...] = k
    v_out[...] = v
    allowed = mask[...]
    outs = []
    for h in range(q.shape[1] // HD):
        at = slice(h * HD, (h + 1) * HD)
        probs = head_probs(q[:, at], k[:, at], allowed)
        outs.append(mm(probs.astype(BF16), v[:, at]))
    attn_out[...] = jnp.concatenate(outs, axis=1).astype(BF16)


def attend(act, wq, wk, wv, cos, sin, mask):
    rows, width = act.shape
    cols = wq.shape[1]
    step = min(256, cols)
    column = pl.BlockSpec((rows, step), lambda i: (0, i))
    whole = lambda shape: pl.BlockSpec(shape, lambda i: (0, 0))
    weight = pl.BlockSpec((width, step), lambda i: (0, i))
    return pl.pallas_call(
        attend_body,
        grid=(cols // step,),
        in_specs=[whole((rows, width)), weight, weight, weight]
        + [whole((rows, step)), whole((rows, step)), whole((rows, rows))],
        out_specs=[column] * 4,
        out_shape=[jax.ShapeDtypeStruct((rows, cols), BF16)] * 4,
        cost_estimate=pl.CostEstimate(
            flops=6 * rows * width * cols + 16 * rows * rows * cols,
            bytes_accessed=2 * rows * width + 6 * width * cols + 8 * rows * cols,
            transcendentals=rows * rows * cols // HD,
        ),
        name="attend",
    )(act, wq, wk, wv, cos, sin, mask)


def attend_back_body(hidden, wo, q_in, k_in, v_in, attn_in, cos, sin, mask, *rest):
    out = rest[-1]
    grad = mm_nt(hidden[...], wo[...]).astype(BF16)
    allowed = mask[...]
    scale = HD ** (-0.5)
    q_all, k_all, v_all, attn = q_in[...], k_in[...], v_in[...], attn_in[...]
    q_list, k_list, v_list = [], [], []
    for h in range(grad.shape[1] // HD):
        at = slice(h * HD, (h + 1) * HD)
        q, k, v, g = q_all[:, at], k_all[:, at], v_all[:, at], grad[:, at]
        probs = head_probs(q, k, allowed)
        v_list.append(mm_tn(probs.astype(BF16), g))
        delta = jnp.sum(g.astype(F32) * attn[:, at].astype(F32), axis=-1, keepdims=True)
        score_grad = (probs * (mm_nt(g, v) - delta) * scale).astype(BF16)
        q_list.append(mm(score_grad, k))
        k_list.append(mm_tn(score_grad, q))
    cosine, back_sine = cos[...], -sin[...]
    out[0] = turn(jnp.concatenate(q_list, axis=1), cosine, back_sine).astype(BF16)
    out[1] = turn(jnp.concatenate(k_list, axis=1), cosine, back_sine).astype(BF16)
    out[2] = jnp.concatenate(v_list, axis=1).astype(BF16)


def attend_back(hidden, wo, q, k, v, attn, cos, sin, mask, after):
    rows, width = hidden.shape
    cols = wo.shape[0]
    step = min(256, cols)
    column = pl.BlockSpec((rows, step), lambda i: (0, i))
    whole = lambda shape: pl.BlockSpec(shape, lambda i: (0, 0))
    return pl.pallas_call(
        attend_back_body,
        grid=(cols // step,),
        in_specs=[whole((rows, width)), pl.BlockSpec((step, width), lambda i: (i, 0))]
        + [column] * 4
        + [whole((rows, step)), whole((rows, step)), whole((rows, rows))]
        + [pl.BlockSpec(memory_space=pl.ANY)] * len(after),
        out_specs=pl.BlockSpec((3, rows, step), lambda i: (0, 0, i)),
        out_shape=jax.ShapeDtypeStruct((3, rows, cols), BF16),
        cost_estimate=pl.CostEstimate(
            flops=2 * rows * width * cols + 40 * rows * rows * cols,
            bytes_accessed=2 * rows * width + 2 * width * cols + 14 * rows * cols,
            transcendentals=rows * rows * cols // HD,
        ),
        name="attend_back",
    )(hidden, wo, q, k, v, attn, cos, sin, mask, *after)


def outer_body(count, has_add, which, *refs):
    total = None
    for c in range(count):
        part = mm_tn(refs[c][...], refs[count + c][...])
        total = part if total is None else total + part
    if has_add:
        total = total + refs[2 * count][...]
    refs[-1][...] = total


def outer(lefts, rights, which, pieces, add=None):
    count = len(lefts)
    piece = lefts[0].shape[1] // pieces
    stacked = rights[0].ndim == 3
    cols = rights[0].shape[-1]
    if stacked:
        step, blocks = cols, rights[0].shape[0]
        right_spec = lambda r: pl.BlockSpec((None, r, step), lambda n, j, w: (n, 0, 0))
    else:
        step = min(1024, cols)
        blocks = cols // step
        right_spec = lambda r: pl.BlockSpec((r, step), lambda n, j, w: (0, n))
    out_spec = pl.BlockSpec((piece, step), lambda n, j, w: (j, n))
    rows = [v.shape[0] for v in lefts]
    out_rows, out_cols = pieces // 2 * piece, blocks * step
    specs = [
        pl.BlockSpec((r, piece), lambda n, j, w: (0, 2 * j + w[0])) for r in rows
    ] + [right_spec(r) for r in rows]
    args = list(lefts) + list(rights)
    if add is not None:
        specs.append(out_spec)
        args.append(add)
    return pl.pallas_call(
        functools.partial(outer_body, count, add is not None),
        grid_spec=pltpu.PrefetchScalarGridSpec(
            num_scalar_prefetch=1,
            grid=(blocks, pieces // 2),
            in_specs=specs,
            out_specs=out_spec,
        ),
        out_shape=jax.ShapeDtypeStruct((out_rows, out_cols), F32),
        cost_estimate=pl.CostEstimate(
            flops=2 * sum(rows) * out_rows * out_cols,
            bytes_accessed=2 * sum(rows) * (out_rows + out_cols) + 4 * out_rows * out_cols,
            transcendentals=0,
        ),
    )(which.reshape(1).astype(jnp.int32), *args)


class Cube:
    def __init__(self, axis, size):
        self.axis = axis
        self.size = size
        self.bits = [1 << i for i in range(size.bit_length() - 1)]
        self.me = lax.axis_index(axis)

    def swap(self, value, bit):
        return lax.ppermute(value, self.axis, [(i, i ^ bit) for i in range(self.size)])

    def bit_of(self, bit):
        return (self.me // bit) % 2

    def own_start(self, rows, bits):
        start = 0
        for bit in bits:
            rows = rows // 2
            start = start + self.bit_of(bit) * rows
        return start

    def scatter(self, make, rows, bits):
        first = True
        value = None
        for bit in bits:
            half = rows // 2
            mine = self.bit_of(bit)
            if first:
                away = make((1 - mine) * half, half)
                got = self.swap(away, bit)
                value = make(mine * half, half) + got
                first = False
            else:
                away = lax.dynamic_slice_in_dim(value, (1 - mine) * half, half, 0)
                got = self.swap(away, bit)
                value = lax.dynamic_slice_in_dim(value, mine * half, half, 0) + got
            rows = half
        return value

    def gather(self, value, bits):
        for bit in reversed(bits):
            got = self.swap(value, bit)
            mine = self.bit_of(bit)
            value = jnp.where(
                mine == 0,
                jnp.concatenate([value, got], axis=0),
                jnp.concatenate([got, value], axis=0),
            )
        return value

    def total(self, value):
        for bit in self.bits:
            value = value + self.swap(value, bit)
        return value


def on_device(sizes):
    dp_size, tensor_size = sizes

    def run(
        block_input,
        block_owner,
        token_mask,
        attention_gain,
        query_weight,
        key_weight,
        value_weight,
        output_weight,
        feedforward_gain,
        gate_weight,
        up_weight,
        down_weight,
        cotangent,
    ):
        row_count, width = block_input.shape
        head_count = query_weight.shape[1] // HD
        head_cols = head_count * HD
        tensor = Cube("tensor", tensor_size)
        data = Cube("dp", dp_size)
        core = data.bit_of(1)
        pair_lists = [[i for i in range(dp_size) if i % 2 == c] for c in range(2)]

        bounds = [(0, FIRST), (FIRST, row_count)]
        orders = (tensor.bits, tensor.bits[::-1])

        def halves(size):
            return [(0, size // 2, orders[0]), (size // 2, size // 2, orders[1])]

        def own_rows(value):
            size = value.shape[0]
            return jnp.concatenate(
                [
                    lax.dynamic_slice_in_dim(
                        value, base + tensor.own_start(rows, bits), rows // tensor_size, 0
                    )
                    for base, rows, bits in halves(size)
                ],
                axis=0,
            )

        def scatter_rows(make, size):
            return jnp.concatenate(
                [
                    tensor.scatter(lambda s, n, base=base: make(base + s, n), rows, bits)
                    for base, rows, bits in halves(size)
                ],
                axis=0,
            )

        def gather_rows(value, size):
            quarter = size // 2 // tensor_size
            return jnp.concatenate(
                [
                    tensor.gather(value[i * quarter : (i + 1) * quarter], bits)
                    for i, (_, _, bits) in enumerate(halves(size))
                ],
                axis=0,
            )

        def rows_of(value, start, size):
            return lax.dynamic_slice_in_dim(value, start, size, 0)

        def core_sum(lefts, rights):
            away = outer(lefts, rights, 1 - core, dp_size)
            got = data.swap(away, 1)
            return outer(lefts, rights, core, dp_size, add=got)

        def z_scatter(value):
            return lax.psum_scatter(
                value, "dp", scatter_dimension=0, tiled=True, axis_index_groups=pair_lists
            )

        first_block = lax.axis_index("dp") * (row_count // BLK)
        owners = jnp.broadcast_to(block_owner[:, None], (row_count // BLK, BLK)).reshape(-1)
        row_index = jnp.arange(row_count, dtype=jnp.int32)
        positions = (row_index // BLK + first_block - owners) * BLK + row_index % BLK
        cosine, sine = rope_tables(positions, HD, min(256, head_cols))

        saved = []
        for lo, hi in bounds:
            size = hi - lo
            x_f = block_input[lo:hi].astype(F32)
            inv_f = lax.rsqrt(jnp.mean(x_f * x_f, axis=-1, keepdims=True) + NORM_EPS)
            act = (x_f * inv_f * attention_gain).astype(BF16)
            rows = jnp.where(
                token_mask[lo:hi, None] > 0, cotangent[lo:hi], jnp.zeros_like(cotangent[lo:hi])
            )
            cos_g, sin_g = cosine[lo:hi], sine[lo:hi]
            own_g, pos_g, mask_g = owners[lo:hi], positions[lo:hi], token_mask[lo:hi]
            allowed = (
                (own_g[:, None] == own_g[None, :])
                & (pos_g[None, :] <= pos_g[:, None])
                & ((mask_g[None, :] > 0) | (pos_g[None, :] == 0))
            ).astype(F32)
            q, k, v, flat = attend(
                act, query_weight, key_weight, value_weight, cos_g, sin_g, allowed
            )
            added = scatter_rows(
                lambda s, n, flat=flat: mm(rows_of(flat, s, n), output_weight), size
            )
            x_own = own_rows(block_input[lo:hi]).astype(F32)
            hid = x_own + added
            inv_two = lax.rsqrt(jnp.mean(hid * hid, axis=-1, keepdims=True) + NORM_EPS)
            unit = gather_rows(hid * inv_two, size)
            act_two = (unit * feedforward_gain).astype(BF16)
            saved.append(
                dict(q=q, k=k, v=v, allowed=allowed, flat=flat, act=act, rows=rows, x_f=x_f,
                     cos=cos_g, sin=sin_g, x_own=x_own, hid=hid, added=added, inv_two=inv_two,
                     act_two=act_two)
            )

        def chunks(key):
            return [s[key] for s in saved]

        for (lo, hi), s in zip(bounds, saved):
            s["gate_pre"] = mm(s["act_two"], gate_weight)
            s["up_pre"] = mm(s["act_two"], up_weight)
            s["sig"] = jax.nn.sigmoid(s["gate_pre"])
            s["inner"] = (s["gate_pre"] * s["sig"] * s["up_pre"]).astype(BF16)
        down_part = core_sum(chunks("rows"), chunks("inner"))
        down_sum = z_scatter(down_part).T

        gain_parts = jnp.zeros((width,), F32)
        for (lo, hi), s in zip(bounds, saved):
            size = hi - lo
            rows = s["rows"]
            inner_grad = mm_nt(rows, down_weight)
            gate_pre, up_pre, sig = s["gate_pre"], s["up_pre"], s["sig"]
            gate_pre, up_pre, _ = lax.optimization_barrier((gate_pre, up_pre, down_part))
            gate_back = (inner_grad * up_pre * sig * (1.0 + gate_pre * (1.0 - sig))).astype(BF16)
            up_back = (inner_grad * gate_pre * sig).astype(BF16)
            s["gate_back"], s["up_back"] = gate_back, up_back
            part = scatter_rows(
                lambda st, n, a=gate_back, b=up_back: mm_nt(rows_of(a, st, n), gate_weight)
                + mm_nt(rows_of(b, st, n), up_weight),
                size,
            )
            s["part"] = part
            unit = s["hid"] * s["inv_two"]
            gain_parts = gain_parts + jnp.sum(part * unit, axis=0)
            scaled = part * feedforward_gain
            back = s["inv_two"] * (
                scaled - unit * jnp.mean(scaled * unit, axis=-1, keepdims=True)
            )
            s["hidden_grad"] = own_rows(rows).astype(F32) + back
            s["hidden_back"] = (rows.astype(F32) + gather_rows(back, size)).astype(BF16)

        gate_part = core_sum(chunks("act_two"), chunks("gate_back"))
        gate_sum = z_scatter(gate_part)
        up_part = core_sum(chunks("act_two"), chunks("up_back"))
        up_sum = z_scatter(up_part)

        outs = []
        for (lo, hi), s in zip(bounds, saved):
            size = hi - lo
            late_inner, _ = lax.optimization_barrier((s["inner"], saved[-1]["part"]))
            mlp = scatter_rows(
                lambda st, n, a=late_inner: mm(rows_of(a, st, n), down_weight), size
            )
            full = gather_rows(s["added"] + mlp, size)
            outs.append((s["x_f"] + full).astype(BF16))
        block_output = jnp.concatenate(outs, axis=0)

        first_parts = jnp.zeros((width,), F32)
        input_grads = []
        for (lo, hi), s in zip(bounds, saved):
            size = hi - lo
            back3 = attend_back(
                s["hidden_back"], output_weight, s["q"], s["k"], s["v"], s["flat"],
                s["cos"], s["sin"], s["allowed"], (down_part, gate_part, up_part),
            )
            s["qkv_back"] = back3
            q_back, k_back, v_back = back3[0], back3[1], back3[2]
            part = scatter_rows(
                lambda st, n, a=q_back, b=k_back, c=v_back: mm_nt(rows_of(a, st, n), query_weight)
                + mm_nt(rows_of(b, st, n), key_weight)
                + mm_nt(rows_of(c, st, n), value_weight),
                size,
            )
            x_own = s["x_own"]
            inv_one = lax.rsqrt(jnp.mean(x_own * x_own, axis=-1, keepdims=True) + NORM_EPS)
            unit = x_own * inv_one
            first_parts = first_parts + jnp.sum(part * unit, axis=0)
            scaled = part * attention_gain
            back = inv_one * (scaled - unit * jnp.mean(scaled * unit, axis=-1, keepdims=True))
            input_grads.append(gather_rows(s["hidden_grad"] + back, size))
        input_gradient = jnp.concatenate(input_grads, axis=0)

        out_sum = z_scatter(core_sum(chunks("hidden_back"), chunks("flat"))).T
        qkv_sum = z_scatter(core_sum(chunks("act"), chunks("qkv_back")))
        query_sum = qkv_sum[:, :head_cols]
        key_sum = qkv_sum[:, head_cols : 2 * head_cols]
        value_sum = qkv_sum[:, 2 * head_cols :]

        gains = data.total(tensor.total(jnp.stack([first_parts, gain_parts])))
        gain_piece = width // dp_size
        gains = lax.dynamic_slice_in_dim(gains, lax.axis_index("dp") * gain_piece, gain_piece, 1)
        return (
            block_output,
            input_gradient,
            gains[0],
            query_sum,
            key_sum,
            value_sum,
            out_sum,
            gains[1],
            gate_sum,
            up_sum,
            down_sum,
        )

    return run


def solution(mesh):
    sizes = (mesh.shape["dp"], mesh.shape["tensor"])
    body = on_device(sizes)

    return jax.shard_map(
        body,
        mesh=mesh,
        in_specs=(
            P("dp", None),
            P("dp"),
            P("dp"),
            P(),
            P(None, "tensor"),
            P(None, "tensor"),
            P(None, "tensor"),
            P("tensor", None),
            P(),
            P(None, "tensor"),
            P(None, "tensor"),
            P("tensor", None),
            P("dp", None),
        ),
        out_specs=(
            P("dp", None),
            P("dp", None),
            P("dp"),
            P("dp", "tensor"),
            P("dp", "tensor"),
            P("dp", "tensor"),
            P("tensor", "dp"),
            P("dp"),
            P("dp", "tensor"),
            P("dp", "tensor"),
            P("tensor", "dp"),
        ),
        check_vma=False,
    )
```

```python
import functools

import jax
import jax.numpy as jnp
from jax import lax
from jax.experimental import pallas as pl
from jax.experimental.pallas import tpu as pltpu
from jax.sharding import PartitionSpec as P


HD = 64
BLK = 128
SEQ_BLOCKS = 4
FIRST = BLK * SEQ_BLOCKS

NORM_EPS = 1e-05
ROPE_BASE = 130000.0
MASKED = -1e30


F32 = jnp.float32
BF16 = jnp.bfloat16


def mm(a, b):
    return jnp.dot(a, b, preferred_element_type=F32)


def mm_nt(a, b):
    return lax.dot_general(a, b, (((1,), (1,)), ((), ())), preferred_element_type=F32)


def mm_tn(a, b):
    return lax.dot_general(a, b, (((0,), (0,)), ((), ())), preferred_element_type=F32)


def rope_tables(positions, lanes):
    half_width = HD // 2
    lane = jnp.arange(lanes, dtype=jnp.int32)
    frequency = ROPE_BASE ** (-((lane % half_width).astype(F32) * 2.0 / HD))
    sign = jnp.where(lane % HD < half_width, -1.0, 1.0).astype(F32)
    angles = positions.astype(F32)[:, None] * frequency[None, :]
    return jnp.cos(angles), jnp.sin(angles) * sign[None, :]


def widen(table, lanes):
    return jnp.concatenate([table] * (lanes // table.shape[1]), axis=1)


def turn(values, cosine, signed_sine):
    lanes = values.shape[1]
    half = HD // 2
    lane = lax.broadcasted_iota(jnp.int32, values.shape, 1)
    other = jnp.where(
        lane % HD < half,
        pltpu.roll(values, lanes - half, 1),
        pltpu.roll(values, half, 1),
    )
    return values * cosine + other * signed_sine


def head_probs(q, k, mask):
    scores = mm_nt(q, k) * HD ** (-0.5)
    scores = jnp.where(mask > 0, scores, MASKED)
    peak = jnp.max(scores, axis=-1, keepdims=True)
    raised = jnp.exp(scores - peak)
    return raised * (1.0 / jnp.sum(raised, axis=-1, keepdims=True))


def attend_body(act, wq, wk, wv, cos, sin, mask, q_out, k_out, v_out, attn_out):
    rows = act[...]
    cosine = widen(cos[...], wq.shape[1])
    sine = widen(sin[...], wq.shape[1])
    q = turn(mm(rows, wq[...]), cosine, sine).astype(BF16)
    k = turn(mm(rows, wk[...]), cosine, sine).astype(BF16)
    v = mm(rows, wv[...]).astype(BF16)
    q_out[...] = q
    k_out[...] = k
    v_out[...] = v
    allowed = mask[...]
    outs = []
    for h in range(q.shape[1] // HD):
        at = slice(h * HD, (h + 1) * HD)
        probs = head_probs(q[:, at], k[:, at], allowed)
        outs.append(mm(probs.astype(BF16), v[:, at]))
    attn_out[...] = jnp.concatenate(outs, axis=1).astype(BF16)


def attend(act, wq, wk, wv, cos, sin, mask):
    rows, width = act.shape
    cols = wq.shape[1]
    step = min(256, cols)
    column = pl.BlockSpec((rows, step), lambda i: (0, i))
    whole = lambda shape: pl.BlockSpec(shape, lambda i: (0, 0))
    weight = pl.BlockSpec((width, step), lambda i: (0, i))
    return pl.pallas_call(
        attend_body,
        grid=(cols // step,),
        in_specs=[whole((rows, width)), weight, weight, weight]
        + [whole(cos.shape), whole(cos.shape), whole((rows, rows))],
        out_specs=[column] * 4,
        out_shape=[jax.ShapeDtypeStruct((rows, cols), BF16)] * 4,
        cost_estimate=pl.CostEstimate(
            flops=6 * rows * width * cols + 16 * rows * rows * cols,
            bytes_accessed=2 * rows * width + 6 * width * cols + 8 * rows * cols,
            transcendentals=rows * rows * cols // HD,
        ),
        name="attend",
    )(act, wq, wk, wv, cos, sin, mask)


def attend_back_body(hidden, wo, q_in, k_in, v_in, attn_in, cos, sin, mask, *rest):
    out = rest[-1]
    grad = mm_nt(hidden[...], wo[...]).astype(BF16)
    allowed = mask[...]
    scale = HD ** (-0.5)
    q_all, k_all, v_all, attn = q_in[...], k_in[...], v_in[...], attn_in[...]
    q_list, k_list, v_list = [], [], []
    for h in range(grad.shape[1] // HD):
        at = slice(h * HD, (h + 1) * HD)
        q, k, v, g = q_all[:, at], k_all[:, at], v_all[:, at], grad[:, at]
        probs = head_probs(q, k, allowed)
        v_list.append(mm_tn(probs.astype(BF16), g))
        delta = jnp.sum(g.astype(F32) * attn[:, at].astype(F32), axis=-1, keepdims=True)
        score_grad = (probs * (mm_nt(g, v) - delta) * scale).astype(BF16)
        q_list.append(mm(score_grad, k))
        k_list.append(mm_tn(score_grad, q))
    cosine, back_sine = widen(cos[...], wo.shape[0]), -widen(sin[...], wo.shape[0])
    out[0] = turn(jnp.concatenate(q_list, axis=1), cosine, back_sine).astype(BF16)
    out[1] = turn(jnp.concatenate(k_list, axis=1), cosine, back_sine).astype(BF16)
    out[2] = jnp.concatenate(v_list, axis=1).astype(BF16)


def attend_back(hidden, wo, q, k, v, attn, cos, sin, mask, after):
    rows, width = hidden.shape
    cols = wo.shape[0]
    step = min(256, cols)
    column = pl.BlockSpec((rows, step), lambda i: (0, i))
    whole = lambda shape: pl.BlockSpec(shape, lambda i: (0, 0))
    return pl.pallas_call(
        attend_back_body,
        grid=(cols // step,),
        in_specs=[whole((rows, width)), pl.BlockSpec((step, width), lambda i: (i, 0))]
        + [column] * 4
        + [whole(cos.shape), whole(cos.shape), whole((rows, rows))]
        + [pl.BlockSpec(memory_space=pl.ANY)] * len(after),
        out_specs=pl.BlockSpec((3, rows, step), lambda i: (0, 0, i)),
        out_shape=jax.ShapeDtypeStruct((3, rows, cols), BF16),
        cost_estimate=pl.CostEstimate(
            flops=2 * rows * width * cols + 40 * rows * rows * cols,
            bytes_accessed=2 * rows * width + 2 * width * cols + 14 * rows * cols,
            transcendentals=rows * rows * cols // HD,
        ),
        name="attend_back",
    )(hidden, wo, q, k, v, attn, cos, sin, mask, *after)


def outer_body(count, has_add, which, *refs):
    lefts = [refs[c][...].T for c in range(count)]
    rights, out = refs[count : 2 * count], refs[-1]
    width = rights[0].shape[-1]
    planes = rights[0].shape[0] if len(rights[0].shape) == 3 else 1
    tile = min(512, width)
    for plane in range(planes):
        for start in range(0, width, tile):
            total = None
            for left, right in zip(lefts, rights):
                at = pl.ds(start, tile)
                block = right[plane, :, at] if len(right.shape) == 3 else right[:, at]
                part = mm(left, block)
                total = part if total is None else total + part
            at = pl.ds(plane * width + start, tile)
            if has_add:
                total = total + refs[2 * count][:, at]
            out[:, at] = total


def outer(lefts, rights, which, pieces, add=None, part=(0, 1)):
    count = len(lefts)
    piece = lefts[0].shape[1] // pieces
    index, parts = part
    rows = [v.shape[0] for v in lefts]
    if rights[0].ndim == 3:
        planes, _, cols = rights[0].shape
        out_cols = planes * cols
        right_specs = [pl.BlockSpec((planes, r, cols), lambda j, w: (0, 0, 0)) for r in rows]
    else:
        out_cols = rights[0].shape[1] // parts
        right_specs = [pl.BlockSpec((r, out_cols), lambda j, w: (0, index)) for r in rows]
    out_spec = pl.BlockSpec((piece, out_cols), lambda j, w: (j, 0))
    out_rows = pieces // 2 * piece
    specs = [pl.BlockSpec((r, piece), lambda j, w: (0, 2 * j + w[0])) for r in rows]
    specs += right_specs
    args = list(lefts) + list(rights)
    if add is not None:
        specs.append(out_spec)
        args.append(add)
    return pl.pallas_call(
        functools.partial(outer_body, count, add is not None),
        grid_spec=pltpu.PrefetchScalarGridSpec(
            num_scalar_prefetch=1,
            grid=(pieces // 2,),
            in_specs=specs,
            out_specs=out_spec,
        ),
        out_shape=jax.ShapeDtypeStruct((out_rows, out_cols), F32),
        cost_estimate=pl.CostEstimate(
            flops=2 * sum(rows) * out_rows * out_cols,
            bytes_accessed=2 * sum(rows) * (out_rows + out_cols) + 4 * out_rows * out_cols,
            transcendentals=0,
        ),
    )(which.reshape(1).astype(jnp.int32), *args)


class Cube:
    def __init__(self, axis, size):
        self.axis = axis
        self.size = size
        self.bits = [1 << i for i in range(size.bit_length() - 1)]
        self.me = lax.axis_index(axis)

    def swap(self, value, bit):
        return lax.ppermute(value, self.axis, [(i, i ^ bit) for i in range(self.size)])

    def bit_of(self, bit):
        return (self.me >> (bit.bit_length() - 1)) & 1

    def own_start(self, rows, bits):
        start = 0
        for bit in bits:
            rows = rows // 2
            start = start + self.bit_of(bit) * rows
        return start

    def scatter(self, value, rows, bits):
        for bit in bits:
            half = rows // 2
            mine = self.bit_of(bit)
            away = lax.dynamic_slice_in_dim(value, (1 - mine) * half, half, 0)
            got = self.swap(away, bit)
            value = lax.dynamic_slice_in_dim(value, mine * half, half, 0) + got
            rows = half
        return value

    def gather(self, value, bits, after):
        for step, bit in enumerate(reversed(bits)):
            last = step == len(bits) - 1
            got = self.swap(value, bit)
            if last and after is not None:
                value, got, _ = lax.optimization_barrier((value, got, after))
            mine = self.bit_of(bit)
            value = jnp.where(
                mine == 0,
                jnp.concatenate([value, got], axis=0),
                jnp.concatenate([got, value], axis=0),
            )
        return value

    def total(self, value):
        for bit in self.bits:
            value = value + self.swap(value, bit)
        return value


def on_device(sizes):
    dp_size, tensor_size = sizes

    def run(
        block_input,
        block_owner,
        token_mask,
        attention_gain,
        query_weight,
        key_weight,
        value_weight,
        output_weight,
        feedforward_gain,
        gate_weight,
        up_weight,
        down_weight,
        cotangent,
    ):
        row_count, width = block_input.shape
        head_count = query_weight.shape[1] // HD
        head_cols = head_count * HD
        tensor = Cube("tensor", tensor_size)
        data = Cube("dp", dp_size)
        core = data.bit_of(1)
        pair_lists = [[i for i in range(dp_size) if i % 2 == c] for c in range(2)]

        bounds = [(0, FIRST), (FIRST, row_count)]
        orders = (tensor.bits, tensor.bits[::-1])

        def halves(size):
            return [(0, size // 2, orders[0]), (size // 2, size // 2, orders[1])]

        def own_rows(value):
            size = value.shape[0]
            return jnp.concatenate(
                [
                    lax.dynamic_slice_in_dim(
                        value, base + tensor.own_start(rows, bits), rows // tensor_size, 0
                    )
                    for base, rows, bits in halves(size)
                ],
                axis=0,
            )

        def scatter_rows(make, size):
            parts = halves(size)
            half = parts[0][1] // 2

            def piece(flip):
                starts = []
                for base, _, bits in parts:
                    mine = tensor.bit_of(bits[0])
                    starts.append(base + (1 - mine if flip else mine) * half)
                return make(starts, half)

            away = piece(True)
            got = [
                tensor.swap(away[i * half : (i + 1) * half], bits[0])
                for i, (_, _, bits) in enumerate(parts)
            ]
            keep = piece(False)
            return jnp.concatenate(
                [
                    tensor.scatter(keep[i * half : (i + 1) * half] + got[i], half, bits[1:])
                    for i, (_, _, bits) in enumerate(parts)
                ],
                axis=0,
            )

        def gather_rows(value, size, after=None):
            quarter = size // 2 // tensor_size
            return jnp.concatenate(
                [
                    tensor.gather(value[i * quarter : (i + 1) * quarter], bits, after)
                    for i, (_, _, bits) in enumerate(halves(size))
                ],
                axis=0,
            )

        def rows_of(value, starts, size):
            return jnp.concatenate(
                [lax.dynamic_slice_in_dim(value, start, size, 0) for start in starts], axis=0
            )

        def core_sum(lefts, rights, part=(0, 1)):
            away = outer(lefts, rights, 1 - core, dp_size, part=part)
            got = data.swap(away, 1)
            return outer(lefts, rights, core, dp_size, add=got, part=part)

        def z_scatter(value):
            return lax.psum_scatter(
                value, "dp", scatter_dimension=0, tiled=True, axis_index_groups=pair_lists
            )

        first_block = lax.axis_index("dp") * (row_count // BLK)
        owners = jnp.broadcast_to(block_owner[:, None], (row_count // BLK, BLK)).reshape(-1)
        row_index = jnp.arange(row_count, dtype=jnp.int32)
        positions = (row_index // BLK + first_block - owners) * BLK + row_index % BLK
        cosine, sine = rope_tables(positions, min(128, head_cols))

        saved = []
        for lo, hi in bounds:
            size = hi - lo
            x_f = block_input[lo:hi].astype(F32)
            inv_f = lax.rsqrt(jnp.mean(x_f * x_f, axis=-1, keepdims=True) + NORM_EPS)
            act = (x_f * inv_f * attention_gain).astype(BF16)
            rows = jnp.where(
                token_mask[lo:hi, None] > 0, cotangent[lo:hi], jnp.zeros_like(cotangent[lo:hi])
            )
            cos_g, sin_g = cosine[lo:hi], sine[lo:hi]
            own_g, pos_g, mask_g = owners[lo:hi], positions[lo:hi], token_mask[lo:hi]
            allowed = (
                (own_g[:, None] == own_g[None, :])
                & (pos_g[None, :] <= pos_g[:, None])
                & ((mask_g[None, :] > 0) | (pos_g[None, :] == 0))
            ).astype(F32)
            q, k, v, flat = attend(
                act, query_weight, key_weight, value_weight, cos_g, sin_g, allowed
            )
            added = scatter_rows(
                lambda s, n, flat=flat: mm(rows_of(flat, s, n), output_weight), size
            )
            x_own = own_rows(block_input[lo:hi]).astype(F32)
            hid = x_own + added
            inv_two = lax.rsqrt(jnp.mean(hid * hid, axis=-1, keepdims=True) + NORM_EPS)
            after = saved[-1]["act_two"] if saved else None
            unit = gather_rows(hid * inv_two, size, after)
            act_two = (unit * feedforward_gain).astype(BF16)
            saved.append(
                dict(q=q, k=k, v=v, allowed=allowed, flat=flat, act=act, rows=rows, x_f=x_f,
                     cos=cos_g, sin=sin_g, x_own=x_own, hid=hid, added=added, inv_two=inv_two,
                     act_two=act_two)
            )

        def chunks(key):
            return [s[key] for s in saved]

        for s in saved:
            s["inner_grad"] = mm_nt(s["rows"], down_weight)
            s["gate_pre"] = mm(s["act_two"], gate_weight)
            s["up_pre"] = mm(s["act_two"], up_weight)
            s["sig"] = jax.nn.sigmoid(s["gate_pre"])
            s["inner"] = (s["gate_pre"] * s["sig"] * s["up_pre"]).astype(BF16)
        down_parts = [core_sum(chunks("rows"), chunks("inner"), (i, 2)) for i in range(2)]
        down_sums = [z_scatter(v) for v in down_parts]

        gain_parts = jnp.zeros((width,), F32)
        for index, ((lo, hi), s) in enumerate(zip(bounds, saved)):
            size = hi - lo
            rows = s["rows"]
            inner_grad = s["inner_grad"]
            gate_pre, up_pre, sig = s["gate_pre"], s["up_pre"], s["sig"]
            gate_pre, up_pre, _ = lax.optimization_barrier((gate_pre, up_pre, down_parts))
            gate_back = (inner_grad * up_pre * sig * (1.0 + gate_pre * (1.0 - sig))).astype(BF16)
            up_back = (inner_grad * gate_pre * sig).astype(BF16)
            s["gate_back"], s["up_back"] = gate_back, up_back
            part = scatter_rows(
                lambda st, n, a=gate_back, b=up_back: mm_nt(rows_of(a, st, n), gate_weight)
                + mm_nt(rows_of(b, st, n), up_weight),
                size,
            )
            s["part"] = part
            unit = s["hid"] * s["inv_two"]
            gain_parts = gain_parts + jnp.sum(part * unit, axis=0)
            scaled = part * feedforward_gain
            back = s["inv_two"] * (
                scaled - unit * jnp.mean(scaled * unit, axis=-1, keepdims=True)
            )
            s["hidden_grad"] = own_rows(rows).astype(F32) + back
            after = saved[index - 1]["hidden_back"] if index else None
            full = gather_rows(back, size, after)
            s["hidden_back"] = (rows.astype(F32) + full).astype(BF16)

        gate_part = core_sum(chunks("act_two"), chunks("gate_back"))
        gate_sum = z_scatter(gate_part)
        up_part = core_sum(chunks("act_two"), chunks("up_back"))
        up_sum = z_scatter(up_part)

        outs = []
        for (lo, hi), s in zip(bounds, saved):
            size = hi - lo
            late_inner, _ = lax.optimization_barrier((s["inner"], saved[-1]["hidden_back"]))
            mlp = scatter_rows(
                lambda st, n, a=late_inner: mm(rows_of(a, st, n), down_weight), size
            )
            full = gather_rows(s["added"] + mlp, size)
            outs.append((s["x_f"] + full).astype(BF16))
        block_output = jnp.concatenate(outs, axis=0)

        first_parts = jnp.zeros((width,), F32)
        input_grads = []
        for (lo, hi), s in zip(bounds, saved):
            size = hi - lo
            back3 = attend_back(
                s["hidden_back"], output_weight, s["q"], s["k"], s["v"], s["flat"],
                s["cos"], s["sin"], s["allowed"], (gate_part, up_part),
            )
            s["qkv_back"] = back3
            q_back, k_back, v_back = back3[0], back3[1], back3[2]
            part = scatter_rows(
                lambda st, n, a=q_back, b=k_back, c=v_back: mm_nt(rows_of(a, st, n), query_weight)
                + mm_nt(rows_of(b, st, n), key_weight)
                + mm_nt(rows_of(c, st, n), value_weight),
                size,
            )
            x_own = s["x_own"]
            inv_one = lax.rsqrt(jnp.mean(x_own * x_own, axis=-1, keepdims=True) + NORM_EPS)
            unit = x_own * inv_one
            first_parts = first_parts + jnp.sum(part * unit, axis=0)
            scaled = part * attention_gain
            back = inv_one * (scaled - unit * jnp.mean(scaled * unit, axis=-1, keepdims=True))
            input_grads.append(gather_rows(s["hidden_grad"] + back, size))
        input_gradient = jnp.concatenate(input_grads, axis=0)

        out_sum = z_scatter(core_sum(chunks("hidden_back"), chunks("flat"))).T
        qkv_part = core_sum(chunks("act"), chunks("qkv_back"))
        qkv_sum = z_scatter(qkv_part)
        down_sums, _ = lax.optimization_barrier((down_sums, qkv_part))
        down_sum = jnp.concatenate([v.T for v in down_sums], axis=0)
        query_sum = qkv_sum[:, :head_cols]
        key_sum = qkv_sum[:, head_cols : 2 * head_cols]
        value_sum = qkv_sum[:, 2 * head_cols :]

        gains = data.total(tensor.total(jnp.stack([first_parts, gain_parts])))
        gain_piece = width // dp_size
        gains = lax.dynamic_slice_in_dim(gains, lax.axis_index("dp") * gain_piece, gain_piece, 1)
        return (
            block_output,
            input_gradient,
            gains[0],
            query_sum,
            key_sum,
            value_sum,
            out_sum,
            gains[1],
            gate_sum,
            up_sum,
            down_sum,
        )

    return run


def solution(mesh):
    sizes = (mesh.shape["dp"], mesh.shape["tensor"])
    body = on_device(sizes)

    return jax.shard_map(
        body,
        mesh=mesh,
        in_specs=(
            P("dp", None),
            P("dp"),
            P("dp"),
            P(),
            P(None, "tensor"),
            P(None, "tensor"),
            P(None, "tensor"),
            P("tensor", None),
            P(),
            P(None, "tensor"),
            P(None, "tensor"),
            P("tensor", None),
            P("dp", None),
        ),
        out_specs=(
            P("dp", None),
            P("dp", None),
            P("dp"),
            P("dp", "tensor"),
            P("dp", "tensor"),
            P("dp", "tensor"),
            P("tensor", "dp"),
            P("dp"),
            P("dp", "tensor"),
            P("dp", "tensor"),
            P("tensor", "dp"),
        ),
        check_vma=False,
    )
```

```python
import functools

import jax
import jax.numpy as jnp
from jax import lax
from jax.experimental import pallas as pl
from jax.experimental.pallas import tpu as pltpu
from jax.sharding import PartitionSpec as P


HD = 64
BLK = 128
SEQ_BLOCKS = 4
FIRST = BLK * SEQ_BLOCKS

NORM_EPS = 1e-05
ROPE_BASE = 130000.0
MASKED = -1e30


F32 = jnp.float32
BF16 = jnp.bfloat16


def mm(a, b):
    return jnp.dot(a, b, preferred_element_type=F32)


def mm_nt(a, b):
    return lax.dot_general(a, b, (((1,), (1,)), ((), ())), preferred_element_type=F32)


def mm_tn(a, b):
    return lax.dot_general(a, b, (((0,), (0,)), ((), ())), preferred_element_type=F32)


def rope_tables(positions, lanes):
    half_width = HD // 2
    lane = jnp.arange(lanes, dtype=jnp.int32)
    frequency = ROPE_BASE ** (-((lane % half_width).astype(F32) * 2.0 / HD))
    sign = jnp.where(lane % HD < half_width, -1.0, 1.0).astype(F32)
    angles = positions.astype(F32)[:, None] * frequency[None, :]
    return jnp.cos(angles), jnp.sin(angles) * sign[None, :]


def widen(table, lanes):
    return jnp.concatenate([table] * (lanes // table.shape[1]), axis=1)


def turn(values, cosine, signed_sine):
    lanes = values.shape[1]
    half = HD // 2
    lane = lax.broadcasted_iota(jnp.int32, values.shape, 1)
    other = jnp.where(
        lane % HD < half,
        pltpu.roll(values, lanes - half, 1),
        pltpu.roll(values, half, 1),
    )
    return values * cosine + other * signed_sine


def head_probs(q, k, mask):
    scores = mm_nt(q, k) * HD ** (-0.5)
    scores = jnp.where(mask > 0, scores, MASKED)
    peak = jnp.max(scores, axis=-1, keepdims=True)
    raised = jnp.exp(scores - peak)
    return raised * (1.0 / jnp.sum(raised, axis=-1, keepdims=True))


def attend_body(x, gain, wq, wk, wv, cos, sin, mask, act_out, q_out, k_out, v_out, attn_out):
    @pl.when(pl.program_id(0) == 0)
    def _():
        values = x[...].astype(F32)
        inverse = lax.rsqrt(jnp.mean(values * values, axis=-1, keepdims=True) + NORM_EPS)
        act_out[...] = (values * inverse * gain[...]).astype(BF16)

    rows = act_out[...]
    cosine = widen(cos[...], wq.shape[1])
    sine = widen(sin[...], wq.shape[1])
    q = turn(mm(rows, wq[...]), cosine, sine).astype(BF16)
    k = turn(mm(rows, wk[...]), cosine, sine).astype(BF16)
    v = mm(rows, wv[...]).astype(BF16)
    q_out[...] = q
    k_out[...] = k
    v_out[...] = v
    count = rows.shape[0]
    tile = min(256, count)
    for start in range(0, count, tile):
        end = start + tile
        allowed = mask[start:end, :end]
        outs = []
        for h in range(q.shape[1] // HD):
            at = slice(h * HD, (h + 1) * HD)
            probs = head_probs(q[start:end, at], k[:end, at], allowed)
            outs.append(mm(probs.astype(BF16), v[:end, at]))
        attn_out[start:end, :] = jnp.concatenate(outs, axis=1).astype(BF16)


def attend(x, gain, wq, wk, wv, cos, sin, mask):
    rows, width = x.shape
    cols = wq.shape[1]
    step = min(256, cols)
    column = pl.BlockSpec((rows, step), lambda i: (0, i))
    whole = lambda shape: pl.BlockSpec(shape, lambda i: (0, 0))
    weight = pl.BlockSpec((width, step), lambda i: (0, i))
    return pl.pallas_call(
        attend_body,
        grid=(cols // step,),
        in_specs=[whole((rows, width)), whole((1, width)), weight, weight, weight]
        + [whole(cos.shape), whole(cos.shape), whole((rows, rows))],
        out_specs=[whole((rows, width))] + [column] * 4,
        out_shape=[jax.ShapeDtypeStruct((rows, width), BF16)]
        + [jax.ShapeDtypeStruct((rows, cols), BF16)] * 4,
        cost_estimate=pl.CostEstimate(
            flops=6 * rows * width * cols + 16 * rows * rows * cols,
            bytes_accessed=4 * rows * width + 6 * width * cols + 8 * rows * cols,
            transcendentals=rows * rows * cols // HD,
        ),
        name="attend",
    )(x, gain.reshape(1, width), wq, wk, wv, cos, sin, mask)


def attend_back_body(hidden, wo, q_in, k_in, v_in, attn_in, cos, sin, mask, *rest):
    out = rest[-1]
    grad = mm_nt(hidden[...], wo[...]).astype(BF16)
    allowed = mask[...]
    scale = HD ** (-0.5)
    q_all, k_all, v_all, attn = q_in[...], k_in[...], v_in[...], attn_in[...]
    q_list, k_list, v_list = [], [], []
    for h in range(grad.shape[1] // HD):
        at = slice(h * HD, (h + 1) * HD)
        q, k, v, g = q_all[:, at], k_all[:, at], v_all[:, at], grad[:, at]
        probs = head_probs(q, k, allowed)
        v_list.append(mm_tn(probs.astype(BF16), g))
        delta = jnp.sum(g.astype(F32) * attn[:, at].astype(F32), axis=-1, keepdims=True)
        score_grad = (probs * (mm_nt(g, v) - delta) * scale).astype(BF16)
        q_list.append(mm(score_grad, k))
        k_list.append(mm_tn(score_grad, q))
    cosine, back_sine = widen(cos[...], wo.shape[0]), -widen(sin[...], wo.shape[0])
    out[0] = turn(jnp.concatenate(q_list, axis=1), cosine, back_sine).astype(BF16)
    out[1] = turn(jnp.concatenate(k_list, axis=1), cosine, back_sine).astype(BF16)
    out[2] = jnp.concatenate(v_list, axis=1).astype(BF16)


def attend_back(hidden, wo, q, k, v, attn, cos, sin, mask, after):
    rows, width = hidden.shape
    cols = wo.shape[0]
    step = min(256, cols)
    column = pl.BlockSpec((rows, step), lambda i: (0, i))
    whole = lambda shape: pl.BlockSpec(shape, lambda i: (0, 0))
    return pl.pallas_call(
        attend_back_body,
        grid=(cols // step,),
        in_specs=[whole((rows, width)), pl.BlockSpec((step, width), lambda i: (i, 0))]
        + [column] * 4
        + [whole(cos.shape), whole(cos.shape), whole((rows, rows))]
        + [pl.BlockSpec(memory_space=pl.ANY)] * len(after),
        out_specs=pl.BlockSpec((3, rows, step), lambda i: (0, 0, i)),
        out_shape=jax.ShapeDtypeStruct((3, rows, cols), BF16),
        cost_estimate=pl.CostEstimate(
            flops=2 * rows * width * cols + 40 * rows * rows * cols,
            bytes_accessed=2 * rows * width + 2 * width * cols + 14 * rows * cols,
            transcendentals=rows * rows * cols // HD,
        ),
        name="attend_back",
    )(hidden, wo, q, k, v, attn, cos, sin, mask, *after)


def outer_body(shape, has_add, which, *refs):
    out, column, at = refs[-1], 0, 0
    adder = refs[-2] if has_add else None
    for count in shape:
        lefts = [refs[at + c][...].T for c in range(count)]
        rights = refs[at + count : at + 2 * count]
        at += 2 * count
        planes = rights[0].shape[0] if len(rights[0].shape) == 3 else 1
        width = rights[0].shape[-1]
        tile = min(512, width)
        for plane in range(planes):
            for start in range(0, width, tile):
                total = None
                for left, right in zip(lefts, rights):
                    span = pl.ds(start, tile)
                    block = right[plane, :, span] if len(right.shape) == 3 else right[:, span]
                    part = mm(left, block)
                    total = part if total is None else total + part
                span = pl.ds(column, tile)
                if has_add:
                    total = total + adder[:, span]
                out[:, span] = total
                column += tile


def outer(groups, which, pieces, add=None, part=(0, 1)):
    piece = groups[0][0][0].shape[1] // pieces
    index, parts = part
    specs, args, out_cols, work, moved = [], [], 0, 0, 0
    for lefts, rights in groups:
        for v in lefts:
            specs.append(pl.BlockSpec((v.shape[0], piece), lambda j, w: (0, 2 * j + w[0])))
            moved += v.size
        for v in rights:
            if v.ndim == 3:
                cols = v.shape[0] * v.shape[2]
                specs.append(pl.BlockSpec(v.shape, lambda j, w: (0, 0, 0)))
            else:
                cols = v.shape[1] // parts
                specs.append(pl.BlockSpec((v.shape[0], cols), lambda j, w: (0, index)))
            moved += v.size // parts * 2
        work += sum(v.shape[0] for v in lefts) * cols
        out_cols += cols
        args += list(lefts) + list(rights)
    out_rows = pieces // 2 * piece
    out_spec = pl.BlockSpec((piece, out_cols), lambda j, w: (j, 0))
    if add is not None:
        specs.append(out_spec)
        args.append(add)
    return pl.pallas_call(
        functools.partial(outer_body, [len(g[0]) for g in groups], add is not None),
        grid_spec=pltpu.PrefetchScalarGridSpec(
            num_scalar_prefetch=1,
            grid=(pieces // 2,),
            in_specs=specs,
            out_specs=out_spec,
        ),
        out_shape=jax.ShapeDtypeStruct((out_rows, out_cols), F32),
        cost_estimate=pl.CostEstimate(
            flops=2 * work * out_rows,
            bytes_accessed=moved + 4 * out_rows * out_cols,
            transcendentals=0,
        ),
    )(which.reshape(1).astype(jnp.int32), *args)


class Cube:
    def __init__(self, axis, size):
        self.axis = axis
        self.size = size
        self.bits = [1 << i for i in range(size.bit_length() - 1)]
        self.me = lax.axis_index(axis)

    def swap(self, value, bit):
        return lax.ppermute(value, self.axis, [(i, i ^ bit) for i in range(self.size)])

    def bit_of(self, bit):
        return (self.me >> (bit.bit_length() - 1)) & 1

    def own_start(self, rows, bits):
        start = 0
        for bit in bits:
            rows = rows // 2
            start = start + self.bit_of(bit) * rows
        return start

    def scatter(self, value, rows, bits):
        for bit in bits:
            half = rows // 2
            mine = self.bit_of(bit)
            away = lax.dynamic_slice_in_dim(value, (1 - mine) * half, half, 0)
            got = self.swap(away, bit)
            value = lax.dynamic_slice_in_dim(value, mine * half, half, 0) + got
            rows = half
        return value

    def gather(self, value, bits, after):
        for step, bit in enumerate(reversed(bits)):
            last = step == len(bits) - 1
            got = self.swap(value, bit)
            if last and after is not None:
                value, got, _ = lax.optimization_barrier((value, got, after))
            mine = self.bit_of(bit)
            value = jnp.where(
                mine == 0,
                jnp.concatenate([value, got], axis=0),
                jnp.concatenate([got, value], axis=0),
            )
        return value

    def total(self, value):
        for bit in self.bits:
            value = value + self.swap(value, bit)
        return value


def on_device(sizes):
    dp_size, tensor_size = sizes

    def run(
        block_input,
        block_owner,
        token_mask,
        attention_gain,
        query_weight,
        key_weight,
        value_weight,
        output_weight,
        feedforward_gain,
        gate_weight,
        up_weight,
        down_weight,
        cotangent,
    ):
        row_count, width = block_input.shape
        head_count = query_weight.shape[1] // HD
        head_cols = head_count * HD
        tensor = Cube("tensor", tensor_size)
        data = Cube("dp", dp_size)
        core = data.bit_of(1)
        pair_lists = [[i for i in range(dp_size) if i % 2 == c] for c in range(2)]

        bounds = [(0, FIRST), (FIRST, row_count)]
        orders = (tensor.bits, tensor.bits[::-1])

        def halves(size):
            return [(0, size // 2, orders[0]), (size // 2, size // 2, orders[1])]

        def own_rows(value):
            size = value.shape[0]
            return jnp.concatenate(
                [
                    lax.dynamic_slice_in_dim(
                        value, base + tensor.own_start(rows, bits), rows // tensor_size, 0
                    )
                    for base, rows, bits in halves(size)
                ],
                axis=0,
            )

        def scatter_rows(make, size):
            parts = halves(size)
            half = parts[0][1] // 2

            def piece(flip):
                starts = []
                for base, _, bits in parts:
                    mine = tensor.bit_of(bits[0])
                    starts.append(base + (1 - mine if flip else mine) * half)
                return make(starts, half)

            away = piece(True)
            got = [
                tensor.swap(away[i * half : (i + 1) * half], bits[0])
                for i, (_, _, bits) in enumerate(parts)
            ]
            keep = piece(False)
            return jnp.concatenate(
                [
                    tensor.scatter(keep[i * half : (i + 1) * half] + got[i], half, bits[1:])
                    for i, (_, _, bits) in enumerate(parts)
                ],
                axis=0,
            )

        def gather_rows(value, size, after=None):
            quarter = size // 2 // tensor_size
            return jnp.concatenate(
                [
                    tensor.gather(value[i * quarter : (i + 1) * quarter], bits, after)
                    for i, (_, _, bits) in enumerate(halves(size))
                ],
                axis=0,
            )

        def rows_of(value, starts, size):
            return jnp.concatenate(
                [lax.dynamic_slice_in_dim(value, start, size, 0) for start in starts], axis=0
            )

        def core_sum(groups, part=(0, 1)):
            away = outer(groups, 1 - core, dp_size, part=part)
            got = data.swap(away, 1)
            return outer(groups, core, dp_size, add=got, part=part)

        def z_scatter(value):
            return lax.psum_scatter(
                value, "dp", scatter_dimension=0, tiled=True, axis_index_groups=pair_lists
            )

        first_block = lax.axis_index("dp") * (row_count // BLK)
        owners = jnp.broadcast_to(block_owner[:, None], (row_count // BLK, BLK)).reshape(-1)
        row_index = jnp.arange(row_count, dtype=jnp.int32)
        positions = (row_index // BLK + first_block - owners) * BLK + row_index % BLK
        cosine, sine = rope_tables(positions, min(128, head_cols))

        saved = []
        for lo, hi in bounds:
            size = hi - lo
            x_f = block_input[lo:hi].astype(F32)
            rows = jnp.where(
                token_mask[lo:hi, None] > 0, cotangent[lo:hi], jnp.zeros_like(cotangent[lo:hi])
            )
            cos_g, sin_g = cosine[lo:hi], sine[lo:hi]
            own_g, pos_g, mask_g = owners[lo:hi], positions[lo:hi], token_mask[lo:hi]
            allowed = (
                (own_g[:, None] == own_g[None, :])
                & (pos_g[None, :] <= pos_g[:, None])
                & ((mask_g[None, :] > 0) | (pos_g[None, :] == 0))
            ).astype(F32)
            act, q, k, v, flat = attend(
                block_input[lo:hi], attention_gain, query_weight, key_weight, value_weight,
                cos_g, sin_g, allowed,
            )
            added = scatter_rows(
                lambda s, n, flat=flat: mm(rows_of(flat, s, n), output_weight), size
            )
            x_own = own_rows(block_input[lo:hi]).astype(F32)
            hid = x_own + added
            inv_two = lax.rsqrt(jnp.mean(hid * hid, axis=-1, keepdims=True) + NORM_EPS)
            after = saved[-1]["act_two"] if saved else None
            unit = gather_rows(hid * inv_two, size, after)
            act_two = (unit * feedforward_gain).astype(BF16)
            saved.append(
                dict(q=q, k=k, v=v, allowed=allowed, flat=flat, act=act, rows=rows, x_f=x_f,
                     cos=cos_g, sin=sin_g, x_own=x_own, hid=hid, added=added, inv_two=inv_two,
                     act_two=act_two)
            )

        def chunks(key):
            return [s[key] for s in saved]

        for s in saved:
            s["inner_grad"] = mm_nt(s["rows"], down_weight)
            s["gate_pre"] = mm(s["act_two"], gate_weight)
            s["up_pre"] = mm(s["act_two"], up_weight)
            s["sig"] = jax.nn.sigmoid(s["gate_pre"])
            s["inner"] = (s["gate_pre"] * s["sig"] * s["up_pre"]).astype(BF16)
        down_parts = [core_sum([(chunks("rows"), chunks("inner"))], (i, 2)) for i in range(2)]
        down_sums = [z_scatter(v) for v in down_parts]

        gain_parts = jnp.zeros((width,), F32)
        for index, ((lo, hi), s) in enumerate(zip(bounds, saved)):
            size = hi - lo
            rows = s["rows"]
            inner_grad = s["inner_grad"]
            gate_pre, up_pre, sig = s["gate_pre"], s["up_pre"], s["sig"]
            if index:
                gate_pre, up_pre, _ = lax.optimization_barrier((gate_pre, up_pre, down_parts))
            gate_back = (inner_grad * up_pre * sig * (1.0 + gate_pre * (1.0 - sig))).astype(BF16)
            up_back = (inner_grad * gate_pre * sig).astype(BF16)
            s["gate_back"], s["up_back"] = gate_back, up_back
            part = scatter_rows(
                lambda st, n, a=gate_back, b=up_back: mm_nt(rows_of(a, st, n), gate_weight)
                + mm_nt(rows_of(b, st, n), up_weight),
                size,
            )
            s["part"] = part
            unit = s["hid"] * s["inv_two"]
            gain_parts = gain_parts + jnp.sum(part * unit, axis=0)
            scaled = part * feedforward_gain
            back = s["inv_two"] * (
                scaled - unit * jnp.mean(scaled * unit, axis=-1, keepdims=True)
            )
            s["hidden_grad"] = own_rows(rows).astype(F32) + back
            after = saved[index - 1]["hidden_back"] if index else None
            full = gather_rows(back, size, after)
            s["hidden_back"] = (rows.astype(F32) + full).astype(BF16)

        both_part = core_sum(
            [(chunks("act_two"), chunks("gate_back")), (chunks("act_two"), chunks("up_back"))],
        )
        both_sum = z_scatter(both_part)

        outs = []
        for s in saved:
            size = s["rows"].shape[0]
            late_inner, _ = lax.optimization_barrier((s["inner"], saved[-1]["part"]))
            mlp = scatter_rows(lambda st, n, a=late_inner: mm(rows_of(a, st, n), down_weight), size)
            full = gather_rows(s["added"] + mlp, size)
            outs.append((s["x_f"] + full).astype(BF16))
        block_output = jnp.concatenate(outs, axis=0)

        first_parts = jnp.zeros((width,), F32)
        input_grads = []
        for (lo, hi), s in zip(bounds, saved):
            size = hi - lo
            back3 = attend_back(
                s["hidden_back"], output_weight, s["q"], s["k"], s["v"], s["flat"],
                s["cos"], s["sin"], s["allowed"], (both_part,),
            )
            s["qkv_back"] = back3
            q_back, k_back, v_back = back3[0], back3[1], back3[2]
            part = scatter_rows(
                lambda st, n, a=q_back, b=k_back, c=v_back: mm_nt(rows_of(a, st, n), query_weight)
                + mm_nt(rows_of(b, st, n), key_weight)
                + mm_nt(rows_of(c, st, n), value_weight),
                size,
            )
            x_own = s["x_own"]
            inv_one = lax.rsqrt(jnp.mean(x_own * x_own, axis=-1, keepdims=True) + NORM_EPS)
            unit = x_own * inv_one
            first_parts = first_parts + jnp.sum(part * unit, axis=0)
            scaled = part * attention_gain
            back = inv_one * (scaled - unit * jnp.mean(scaled * unit, axis=-1, keepdims=True))
            input_grads.append(gather_rows(s["hidden_grad"] + back, size))
        input_gradient = jnp.concatenate(input_grads, axis=0)

        last_part = core_sum(
            [(chunks("act"), chunks("qkv_back")), (chunks("hidden_back"), chunks("flat"))]
        )
        last_sum = z_scatter(last_part)
        down_sums, both_sum, _ = lax.optimization_barrier((down_sums, both_sum, last_part))
        down_sum = jnp.concatenate([v.T for v in down_sums], axis=0)
        ff_cols = gate_weight.shape[1]
        gate_sum, up_sum = both_sum[:, :ff_cols], both_sum[:, ff_cols:]
        query_sum = last_sum[:, :head_cols]
        key_sum = last_sum[:, head_cols : 2 * head_cols]
        value_sum = last_sum[:, 2 * head_cols : 3 * head_cols]
        out_sum = last_sum[:, 3 * head_cols :].T

        gains = data.total(tensor.total(jnp.stack([first_parts, gain_parts])))
        gain_piece = width // dp_size
        gains = lax.dynamic_slice_in_dim(gains, lax.axis_index("dp") * gain_piece, gain_piece, 1)
        return (
            block_output,
            input_gradient,
            gains[0],
            query_sum,
            key_sum,
            value_sum,
            out_sum,
            gains[1],
            gate_sum,
            up_sum,
            down_sum,
        )

    return run


def solution(mesh):
    sizes = (mesh.shape["dp"], mesh.shape["tensor"])
    body = on_device(sizes)

    return jax.shard_map(
        body,
        mesh=mesh,
        in_specs=(
            P("dp", None),
            P("dp"),
            P("dp"),
            P(),
            P(None, "tensor"),
            P(None, "tensor"),
            P(None, "tensor"),
            P("tensor", None),
            P(),
            P(None, "tensor"),
            P(None, "tensor"),
            P("tensor", None),
            P("dp", None),
        ),
        out_specs=(
            P("dp", None),
            P("dp", None),
            P("dp"),
            P("dp", "tensor"),
            P("dp", "tensor"),
            P("dp", "tensor"),
            P("tensor", "dp"),
            P("dp"),
            P("dp", "tensor"),
            P("dp", "tensor"),
            P("tensor", "dp"),
        ),
        check_vma=False,
    )
```

```python
import functools
from types import SimpleNamespace

import jax
import jax.numpy as jnp
from jax import lax
from jax.experimental import pallas as pl
from jax.experimental.pallas import tpu as pltpu
from jax.sharding import PartitionSpec as P


HD = 64
BLK = 128
SEQ_BLOCKS = 4
FIRST = BLK * SEQ_BLOCKS

NORM_EPS = 1e-05
ROPE_BASE = 130000.0
MASKED = -1e30


DP, TP = "dp", "tensor"

F32 = jnp.float32
BF16 = jnp.bfloat16


def mm(a, b):
    return jnp.dot(a, b, preferred_element_type=F32)


def mm_nt(a, b):
    return lax.dot_general(a, b, (((1,), (1,)), ((), ())), preferred_element_type=F32)


def mm_tn(a, b):
    return lax.dot_general(a, b, (((0,), (0,)), ((), ())), preferred_element_type=F32)


def rope_tables(positions, lanes):
    half_width = HD // 2
    lane = jnp.arange(lanes, dtype=jnp.int32)
    frequency = ROPE_BASE ** (-((lane % half_width).astype(F32) * 2.0 / HD))
    sign = jnp.where(lane % HD < half_width, -1.0, 1.0).astype(F32)
    angles = positions.astype(F32)[:, None] * frequency[None, :]
    return jnp.cos(angles), jnp.sin(angles) * sign[None, :]


def widen(table, lanes):
    return jnp.concatenate([table] * (lanes // table.shape[1]), axis=1)


def turn(values, cosine, signed_sine):
    lanes = values.shape[1]
    half = HD // 2
    lane = lax.broadcasted_iota(jnp.int32, values.shape, 1)
    other = jnp.where(
        lane % HD < half,
        pltpu.roll(values, lanes - half, 1),
        pltpu.roll(values, half, 1),
    )
    return values * cosine + other * signed_sine


def head_probs(q, k, mask):
    scores = mm_nt(q, k) * HD ** (-0.5)
    scores = jnp.where(mask > 0, scores, MASKED)
    peak = jnp.max(scores, axis=-1, keepdims=True)
    raised = jnp.exp(scores - peak)
    return raised * (1.0 / jnp.sum(raised, axis=-1, keepdims=True))


def attend_body(x, gain, wq, wk, wv, cos, sin, mask, act_out, q_out, k_out, v_out, attn_out):
    @pl.when(pl.program_id(0) == 0)
    def _():
        values = x[...].astype(F32)
        inverse = lax.rsqrt(jnp.mean(values * values, axis=-1, keepdims=True) + NORM_EPS)
        act_out[...] = (values * inverse * gain[...]).astype(BF16)

    rows = act_out[...]
    cosine = widen(cos[...], wq.shape[1])
    sine = widen(sin[...], wq.shape[1])
    q = turn(mm(rows, wq[...]), cosine, sine).astype(BF16)
    k = turn(mm(rows, wk[...]), cosine, sine).astype(BF16)
    v = mm(rows, wv[...]).astype(BF16)
    q_out[...] = q
    k_out[...] = k
    v_out[...] = v
    count = rows.shape[0]
    tile = min(256, count)
    for start in range(0, count, tile):
        end = start + tile
        allowed = mask[start:end, :end]
        outs = []
        for h in range(q.shape[1] // HD):
            at = slice(h * HD, (h + 1) * HD)
            probs = head_probs(q[start:end, at], k[:end, at], allowed)
            outs.append(mm(probs.astype(BF16), v[:end, at]))
        attn_out[start:end, :] = jnp.concatenate(outs, axis=1).astype(BF16)


def attend(x, row_block, gain, wq, wk, wv, cos, sin, mask):
    rows, width = mask.shape[0], x.shape[1]
    cols = wq.shape[1]
    step = min(256, cols)
    column = pl.BlockSpec((rows, step), lambda i: (0, i))
    whole = lambda shape: pl.BlockSpec(shape, lambda i: (0, 0))
    chunk = lambda v: pl.BlockSpec((rows, v.shape[1]), lambda i: (row_block, 0))
    weight = pl.BlockSpec((width, step), lambda i: (0, i))
    return pl.pallas_call(
        attend_body,
        grid=(cols // step,),
        in_specs=[chunk(x), whole((1, width)), weight, weight, weight]
        + [chunk(cos), chunk(sin), whole((rows, rows))],
        out_specs=[whole((rows, width))] + [column] * 4,
        out_shape=[jax.ShapeDtypeStruct((rows, width), BF16)]
        + [jax.ShapeDtypeStruct((rows, cols), BF16)] * 4,
        cost_estimate=pl.CostEstimate(
            flops=6 * rows * width * cols + 16 * rows * rows * cols,
            bytes_accessed=4 * rows * width + 6 * width * cols + 8 * rows * cols,
            transcendentals=rows * rows * cols // HD,
        ),
    )(x, gain.reshape(1, width), wq, wk, wv, cos, sin, mask)


def attend_back_body(hidden, wo, q_in, k_in, v_in, attn_in, cos, sin, mask, *rest):
    out = rest[-1]
    grad = mm_nt(hidden[...], wo[...]).astype(BF16)
    allowed = mask[...]
    scale = HD ** (-0.5)
    q_all, k_all, v_all, attn = q_in[...], k_in[...], v_in[...], attn_in[...]
    q_list, k_list, v_list = [], [], []
    for h in range(grad.shape[1] // HD):
        at = slice(h * HD, (h + 1) * HD)
        q, k, v, g = q_all[:, at], k_all[:, at], v_all[:, at], grad[:, at]
        probs = head_probs(q, k, allowed)
        v_list.append(mm_tn(probs.astype(BF16), g))
        delta = jnp.sum(g.astype(F32) * attn[:, at].astype(F32), axis=-1, keepdims=True)
        score_grad = (probs * (mm_nt(g, v) - delta) * scale).astype(BF16)
        q_list.append(mm(score_grad, k))
        k_list.append(mm_tn(score_grad, q))
    cosine, back_sine = widen(cos[...], wo.shape[0]), -widen(sin[...], wo.shape[0])
    out[0] = turn(jnp.concatenate(q_list, axis=1), cosine, back_sine).astype(BF16)
    out[1] = turn(jnp.concatenate(k_list, axis=1), cosine, back_sine).astype(BF16)
    out[2] = jnp.concatenate(v_list, axis=1).astype(BF16)


def attend_back(hidden, row_block, wo, q, k, v, attn, cos, sin, mask, after):
    rows, width = hidden.shape
    cols = wo.shape[0]
    step = min(256, cols)
    column = pl.BlockSpec((rows, step), lambda i: (0, i))
    whole = lambda shape: pl.BlockSpec(shape, lambda i: (0, 0))
    chunk = lambda v: pl.BlockSpec((rows, v.shape[1]), lambda i: (row_block, 0))
    return pl.pallas_call(
        attend_back_body,
        grid=(cols // step,),
        in_specs=[whole((rows, width)), pl.BlockSpec((step, width), lambda i: (i, 0))]
        + [column] * 4
        + [chunk(cos), chunk(sin), whole((rows, rows))]
        + [pl.BlockSpec(memory_space=pl.ANY)] * len(after),
        out_specs=pl.BlockSpec((3, rows, step), lambda i: (0, 0, i)),
        out_shape=jax.ShapeDtypeStruct((3, rows, cols), BF16),
        cost_estimate=pl.CostEstimate(
            flops=2 * rows * width * cols + 40 * rows * rows * cols,
            bytes_accessed=2 * rows * width + 2 * width * cols + 14 * rows * cols,
            transcendentals=rows * rows * cols // HD,
        ),
    )(hidden, wo, q, k, v, attn, cos, sin, mask, *after)


def flip_body(value, keep, out):
    kept = jnp.where(keep[...] > 0, value[...].astype(F32), 0.0)
    out[...] = kept.astype(BF16).T


def flip_rows(value, keep):
    rows, width = value.shape
    step = min(512, width)
    return pl.pallas_call(
        flip_body,
        grid=(width // step,),
        in_specs=[
            pl.BlockSpec((rows, step), lambda i: (0, i)),
            pl.BlockSpec((rows, 1), lambda i: (0, 0)),
        ],
        out_specs=pl.BlockSpec((step, rows), lambda i: (i, 0)),
        out_shape=jax.ShapeDtypeStruct((width, rows), BF16),
        cost_estimate=pl.CostEstimate(
            flops=rows * width, bytes_accessed=4 * rows * width, transcendentals=0
        ),
    )(value, keep.reshape(rows, 1))


def outer_body(shape, has_add, flipped, which, *refs):
    out, column, at = refs[-1], 0, 0
    adder = refs[-2] if has_add else None
    for count in shape:
        if flipped:
            rights = refs[at + 1 : at + 1 + count]
            lefts, start = [], 0
            for right in rights:
                lefts.append(refs[at][:, start : start + right.shape[0]])
                start += right.shape[0]
            at += 1 + count
        else:
            lefts = [refs[at + c][...].T for c in range(count)]
            rights = refs[at + count : at + 2 * count]
            at += 2 * count
        planes = rights[0].shape[0] if len(rights[0].shape) == 3 else 1
        width = rights[0].shape[-1]
        tile = min(512, width)
        for plane in range(planes):
            for start in range(0, width, tile):
                total = None
                for left, right in zip(lefts, rights):
                    span = pl.ds(start, tile)
                    block = right[plane, :, span] if len(right.shape) == 3 else right[:, span]
                    part = mm(left, block)
                    total = part if total is None else total + part
                span = pl.ds(column, tile)
                if has_add:
                    total = total + adder[:, span]
                out[:, span] = total
                column += tile


def outer(groups, which, pieces, add=None, part=(0, 1), flipped=False):
    piece = groups[0][0][0].shape[0 if flipped else 1] // pieces
    index, parts = part
    specs, args, out_cols, work, moved = [], [], 0, 0, 0
    for lefts, rights in groups:
        for v in lefts:
            if flipped:
                specs.append(pl.BlockSpec((piece, v.shape[1]), lambda j, w: (2 * j + w[0], 0)))
            else:
                specs.append(pl.BlockSpec((v.shape[0], piece), lambda j, w: (0, 2 * j + w[0])))
            moved += v.size
        for v in rights:
            if v.ndim == 3:
                cols = v.shape[0] * v.shape[2]
                specs.append(pl.BlockSpec(v.shape, lambda j, w: (0, 0, 0)))
            else:
                cols = v.shape[1] // parts
                specs.append(pl.BlockSpec((v.shape[0], cols), lambda j, w: (0, index)))
            moved += v.size // parts * 2
        work += sum(v.shape[-2] for v in rights) * cols
        out_cols += cols
        args += list(lefts) + list(rights)
    out_rows = pieces // 2 * piece
    out_spec = pl.BlockSpec((piece, out_cols), lambda j, w: (j, 0))
    if add is not None:
        specs.append(out_spec)
        args.append(add)
    return pl.pallas_call(
        functools.partial(outer_body, [len(g[1]) for g in groups], add is not None, flipped),
        grid_spec=pltpu.PrefetchScalarGridSpec(
            num_scalar_prefetch=1,
            grid=(pieces // 2,),
            in_specs=specs,
            out_specs=out_spec,
        ),
        out_shape=jax.ShapeDtypeStruct((out_rows, out_cols), F32),
        cost_estimate=pl.CostEstimate(
            flops=2 * work * out_rows,
            bytes_accessed=moved + 4 * out_rows * out_cols,
            transcendentals=0,
        ),
        name="outer",
    )(which.reshape(1).astype(jnp.int32), *args)


class Cube:
    def __init__(self, axis, size):
        self.axis = axis
        self.size = size
        self.bits = [1 << i for i in range(size.bit_length() - 1)]
        self.me = lax.axis_index(axis)

    def swap(self, value, bit):
        return lax.ppermute(value, self.axis, [(i, i ^ bit) for i in range(self.size)])

    def bit_of(self, bit):
        return (self.me >> (bit.bit_length() - 1)) & 1

    def own_start(self, rows, bits):
        start = 0
        for bit in bits:
            rows = rows // 2
            start = start + self.bit_of(bit) * rows
        return start

    def scatter(self, value, rows, bits):
        for bit in bits:
            half = rows // 2
            mine = self.bit_of(bit)
            away = lax.dynamic_slice_in_dim(value, (1 - mine) * half, half, 0)
            got = self.swap(away, bit)
            value = lax.dynamic_slice_in_dim(value, mine * half, half, 0) + got
            rows = half
        return value

    def gather(self, value, bits, after):
        for step, bit in enumerate(reversed(bits)):
            last = step == len(bits) - 1
            got = self.swap(value, bit)
            if last and after is not None:
                value, got, _ = lax.optimization_barrier((value, got, after))
            mine = self.bit_of(bit)
            value = jnp.where(
                mine == 0,
                jnp.concatenate([value, got], axis=0),
                jnp.concatenate([got, value], axis=0),
            )
        return value

    def total(self, value):
        for bit in self.bits:
            value = value + self.swap(value, bit)
        return value


def on_device(sizes):
    dp_size, tensor_size = sizes

    def run(
        block_input,
        block_owner,
        token_mask,
        attention_gain,
        query_weight,
        key_weight,
        value_weight,
        output_weight,
        feedforward_gain,
        gate_weight,
        up_weight,
        down_weight,
        cotangent,
    ):
        row_count, width = block_input.shape
        head_count = query_weight.shape[1] // HD
        head_cols = head_count * HD
        tensor = Cube(TP, tensor_size)
        data = Cube(DP, dp_size)
        core = data.bit_of(1)
        pair_lists = [[i for i in range(dp_size) if i % 2 == c] for c in range(2)]

        bounds = [(0, FIRST), (FIRST, row_count)]
        orders = (tensor.bits, tensor.bits[::-1])

        def halves(size):
            return [(0, size // 2, orders[0]), (size // 2, size // 2, orders[1])]

        def own_rows(value):
            size = value.shape[0]
            return jnp.concatenate(
                [
                    lax.dynamic_slice_in_dim(
                        value, base + tensor.own_start(rows, bits), rows // tensor_size, 0
                    )
                    for base, rows, bits in halves(size)
                ],
                axis=0,
            )

        def scatter_rows(make, size):
            parts = halves(size)
            half = parts[0][1] // 2

            def piece(flip):
                starts = []
                for base, _, bits in parts:
                    mine = tensor.bit_of(bits[0])
                    starts.append(base + (1 - mine if flip else mine) * half)
                return make(starts, half)

            away = piece(True)
            got = [
                tensor.swap(away[i * half : (i + 1) * half], bits[0])
                for i, (_, _, bits) in enumerate(parts)
            ]
            keep = piece(False)
            return jnp.concatenate(
                [
                    tensor.scatter(keep[i * half : (i + 1) * half] + got[i], half, bits[1:])
                    for i, (_, _, bits) in enumerate(parts)
                ],
                axis=0,
            )

        def gather_rows(value, size, after=None):
            quarter = size // 2 // tensor_size
            return jnp.concatenate(
                [
                    tensor.gather(value[i * quarter : (i + 1) * quarter], bits, after)
                    for i, (_, _, bits) in enumerate(halves(size))
                ],
                axis=0,
            )

        def rows_of(value, starts, size):
            return jnp.concatenate(
                [lax.dynamic_slice_in_dim(value, start, size, 0) for start in starts], axis=0
            )

        def core_sum(groups, part=(0, 1), flipped=False):
            away = outer(groups, 1 - core, dp_size, part=part, flipped=flipped)
            got = data.swap(away, 1)
            return outer(groups, core, dp_size, add=got, part=part, flipped=flipped)

        def z_scatter(value):
            return lax.psum_scatter(
                value, DP, scatter_dimension=0, tiled=True, axis_index_groups=pair_lists
            )

        first_block = lax.axis_index(DP) * (row_count // BLK)
        owners = jnp.broadcast_to(block_owner[:, None], (row_count // BLK, BLK)).reshape(-1)
        row_index = jnp.arange(row_count, dtype=jnp.int32)
        positions = (row_index // BLK + first_block - owners) * BLK + row_index % BLK
        cosine, sine = rope_tables(positions, min(128, head_cols))

        saved = []
        for lo, hi in bounds:
            size = hi - lo
            x_f = block_input[lo:hi].astype(F32)
            rows = jnp.where(
                token_mask[lo:hi, None] > 0, cotangent[lo:hi], jnp.zeros_like(cotangent[lo:hi])
            )
            aligned = lo % size == 0
            cut = (lambda v: v) if aligned else (lambda v, lo=lo, hi=hi: v[lo:hi])
            row_block = lo // size if aligned else 0
            cos_g, sin_g = cut(cosine), cut(sine)
            own_g, pos_g, mask_g = owners[lo:hi], positions[lo:hi], token_mask[lo:hi]
            allowed = (
                (own_g[:, None] == own_g[None, :])
                & (pos_g[None, :] <= pos_g[:, None])
                & ((mask_g[None, :] > 0) | (pos_g[None, :] == 0))
            ).astype(F32)
            act, q, k, v, flat = attend(
                cut(block_input), row_block, attention_gain, query_weight, key_weight, value_weight,
                cos_g, sin_g, allowed,
            )
            added = scatter_rows(
                lambda s, n, flat=flat: mm(rows_of(flat, s, n), output_weight), size
            )
            x_own = own_rows(block_input[lo:hi]).astype(F32)
            hid = x_own + added
            inv_two = lax.rsqrt(jnp.mean(hid * hid, axis=-1, keepdims=True) + NORM_EPS)
            after = saved[-1].act_two if saved else None
            unit = gather_rows(hid * inv_two, size, after)
            act_two = (unit * feedforward_gain).astype(BF16)
            saved.append(
                SimpleNamespace(q=q, k=k, v=v, allowed=allowed, flat=flat, act=act, rows=rows, x_f=x_f,
                     cos=cos_g, sin=sin_g, row_block=row_block, x_own=x_own, hid=hid, added=added, inv_two=inv_two,
                     act_two=act_two)
            )

        for s in saved:
            s.inner_grad = mm_nt(s.rows, down_weight)
            s.gate_pre = mm(s.act_two, gate_weight)
            s.up_pre = mm(s.act_two, up_weight)
            s.sig = jax.nn.sigmoid(s.gate_pre)
            s.inner = (s.gate_pre * s.sig * s.up_pre).astype(BF16)
        flipped_rows = flip_rows(cotangent, token_mask)
        down_parts = [
            core_sum([([flipped_rows], [s.inner for s in saved])], (i, 2), True)
            for i in range(2)
        ]
        down_sums = [z_scatter(v) for v in down_parts]

        gain_parts = jnp.zeros((width,), F32)
        for index, ((lo, hi), s) in enumerate(zip(bounds, saved)):
            size = hi - lo
            rows = s.rows
            inner_grad = s.inner_grad
            gate_pre, up_pre, sig = s.gate_pre, s.up_pre, s.sig
            if index:
                gate_pre, up_pre, _ = lax.optimization_barrier((gate_pre, up_pre, down_parts))
            gate_back = (inner_grad * up_pre * sig * (1.0 + gate_pre * (1.0 - sig))).astype(BF16)
            up_back = (inner_grad * gate_pre * sig).astype(BF16)
            s.gate_back, s.up_back = gate_back, up_back
            part = scatter_rows(
                lambda st, n, a=gate_back, b=up_back: mm_nt(rows_of(a, st, n), gate_weight)
                + mm_nt(rows_of(b, st, n), up_weight),
                size,
            )
            s.part = part
            unit = s.hid * s.inv_two
            gain_parts = gain_parts + jnp.sum(part * unit, axis=0)
            scaled = part * feedforward_gain
            back = s.inv_two * (
                scaled - unit * jnp.mean(scaled * unit, axis=-1, keepdims=True)
            )
            s.hidden_grad = own_rows(rows).astype(F32) + back
            after = saved[index - 1].hidden_back if index else None
            full = gather_rows(back, size, after)
            s.hidden_back = (rows.astype(F32) + full).astype(BF16)

        both_part = core_sum(
            [([s.act_two for s in saved], [s.gate_back for s in saved]), ([s.act_two for s in saved], [s.up_back for s in saved])],
        )
        both_sum = z_scatter(both_part)

        outs = []
        for s in saved:
            size = s.rows.shape[0]
            late_inner, _ = lax.optimization_barrier((s.inner, saved[-1].part))
            mlp = scatter_rows(lambda st, n, a=late_inner: mm(rows_of(a, st, n), down_weight), size)
            full = gather_rows(s.added + mlp, size)
            outs.append((s.x_f + full).astype(BF16))
        block_output = jnp.concatenate(outs, axis=0)

        first_parts = jnp.zeros((width,), F32)
        input_grads = []
        for (lo, hi), s in zip(bounds, saved):
            size = hi - lo
            back3 = attend_back(
                s.hidden_back, s.row_block, output_weight, s.q, s.k, s.v, s.flat,
                s.cos, s.sin, s.allowed, (both_part,),
            )
            s.qkv_back = back3
            q_back, k_back, v_back = back3[0], back3[1], back3[2]
            part = scatter_rows(
                lambda st, n, a=q_back, b=k_back, c=v_back: mm_nt(rows_of(a, st, n), query_weight)
                + mm_nt(rows_of(b, st, n), key_weight)
                + mm_nt(rows_of(c, st, n), value_weight),
                size,
            )
            x_own = s.x_own
            inv_one = lax.rsqrt(jnp.mean(x_own * x_own, axis=-1, keepdims=True) + NORM_EPS)
            unit = x_own * inv_one
            first_parts = first_parts + jnp.sum(part * unit, axis=0)
            scaled = part * attention_gain
            back = inv_one * (scaled - unit * jnp.mean(scaled * unit, axis=-1, keepdims=True))
            input_grads.append(gather_rows(s.hidden_grad + back, size))
        input_gradient = jnp.concatenate(input_grads, axis=0)

        last_part = core_sum(
            [([s.act for s in saved], [s.qkv_back for s in saved]), ([s.hidden_back for s in saved], [s.flat for s in saved])]
        )
        last_sum = z_scatter(last_part)
        down_sums, both_sum, _ = lax.optimization_barrier((down_sums, both_sum, last_part))
        down_sum = jnp.concatenate([v.T for v in down_sums], axis=0)
        ff_cols = gate_weight.shape[1]
        gate_sum, up_sum = both_sum[:, :ff_cols], both_sum[:, ff_cols:]
        query_sum = last_sum[:, :head_cols]
        key_sum = last_sum[:, head_cols : 2 * head_cols]
        value_sum = last_sum[:, 2 * head_cols : 3 * head_cols]
        out_sum = last_sum[:, 3 * head_cols :].T

        gains = data.total(tensor.total(jnp.stack([first_parts, gain_parts])))
        gain_piece = width // dp_size
        gains = lax.dynamic_slice_in_dim(gains, lax.axis_index(DP) * gain_piece, gain_piece, 1)
        return (
            block_output,
            input_gradient,
            gains[0],
            query_sum,
            key_sum,
            value_sum,
            out_sum,
            gains[1],
            gate_sum,
            up_sum,
            down_sum,
        )

    return run


def solution(mesh):
    sizes = (mesh.shape[DP], mesh.shape[TP])
    body = on_device(sizes)

    return jax.shard_map(
        body,
        mesh=mesh,
        in_specs=(
            P(DP, None),
            P(DP),
            P(DP),
            P(),
            P(None, TP),
            P(None, TP),
            P(None, TP),
            P(TP, None),
            P(),
            P(None, TP),
            P(None, TP),
            P(TP, None),
            P(DP, None),
        ),
        out_specs=(
            P(DP, None),
            P(DP, None),
            P(DP),
            P(DP, TP),
            P(DP, TP),
            P(DP, TP),
            P(TP, DP),
            P(DP),
            P(DP, TP),
            P(DP, TP),
            P(TP, DP),
        ),
        check_vma=False,
    )
```

```python
import functools
from types import SimpleNamespace

import jax
import jax.numpy as jnp
from jax import lax
from jax.experimental import pallas as pl
from jax.experimental.pallas import tpu as pltpu
from jax.sharding import PartitionSpec as P


HD = 64
BLK = 128
SEQ_BLOCKS = 4
FIRST = BLK * SEQ_BLOCKS

NORM_EPS = 1e-05
ROPE_BASE = 130000.0
MASKED = -1e30


DP, TP = "dp", "tensor"

F32 = jnp.float32
BF16 = jnp.bfloat16


def mm(a, b):
    return jnp.dot(a, b, preferred_element_type=F32)


def mm_nt(a, b):
    return lax.dot_general(a, b, (((1,), (1,)), ((), ())), preferred_element_type=F32)


def mm_tn(a, b):
    return lax.dot_general(a, b, (((0,), (0,)), ((), ())), preferred_element_type=F32)


def rope_tables(positions, lanes):
    half_width = HD // 2
    lane = jnp.arange(lanes, dtype=jnp.int32)
    frequency = ROPE_BASE ** (-((lane % half_width).astype(F32) * 2.0 / HD))
    sign = jnp.where(lane % HD < half_width, -1.0, 1.0).astype(F32)
    angles = positions.astype(F32)[:, None] * frequency[None, :]
    return jnp.cos(angles), jnp.sin(angles) * sign[None, :]


def widen(table, lanes):
    return jnp.concatenate([table] * (lanes // table.shape[1]), axis=1)


def turn(values, cosine, signed_sine):
    lanes = values.shape[1]
    half = HD // 2
    lane = lax.broadcasted_iota(jnp.int32, values.shape, 1)
    other = jnp.where(
        lane % HD < half,
        pltpu.roll(values, lanes - half, 1),
        pltpu.roll(values, half, 1),
    )
    return values * cosine + other * signed_sine


def head_probs(q, k, mask):
    scores = mm_nt(q, k) * HD ** (-0.5)
    scores = jnp.where(mask > 0, scores, MASKED)
    peak = jnp.max(scores, axis=-1, keepdims=True)
    raised = jnp.exp(scores - peak)
    return raised * (1.0 / jnp.sum(raised, axis=-1, keepdims=True))


def attend_body(x, gain, wq, wk, wv, cos, sin, mask, act_out, q_out, k_out, v_out, attn_out):
    @pl.when(pl.program_id(0) == 0)
    def _():
        values = x[...].astype(F32)
        inverse = lax.rsqrt(jnp.mean(values * values, axis=-1, keepdims=True) + NORM_EPS)
        act_out[...] = (values * inverse * gain[...]).astype(BF16)

    rows = act_out[...]
    cosine = widen(cos[...], wq.shape[1])
    sine = widen(sin[...], wq.shape[1])
    q = turn(mm(rows, wq[...]), cosine, sine).astype(BF16)
    k = turn(mm(rows, wk[...]), cosine, sine).astype(BF16)
    v = mm(rows, wv[...]).astype(BF16)
    q_out[...] = q
    k_out[...] = k
    v_out[...] = v
    count = rows.shape[0]
    tile = min(256, count)
    for start in range(0, count, tile):
        end = start + tile
        allowed = mask[start:end, :end]
        outs = []
        for h in range(q.shape[1] // HD):
            at = slice(h * HD, (h + 1) * HD)
            probs = head_probs(q[start:end, at], k[:end, at], allowed)
            outs.append(mm(probs.astype(BF16), v[:end, at]))
        attn_out[start:end, :] = jnp.concatenate(outs, axis=1).astype(BF16)


def attend(x, row_block, gain, wq, wk, wv, cos, sin, mask):
    rows, width = mask.shape[0], x.shape[1]
    cols = wq.shape[1]
    step = min(256, cols)
    column = pl.BlockSpec((rows, step), lambda i: (0, i))
    whole = lambda shape: pl.BlockSpec(shape, lambda i: (0, 0))
    chunk = lambda v: pl.BlockSpec((rows, v.shape[1]), lambda i: (row_block, 0))
    weight = pl.BlockSpec((width, step), lambda i: (0, i))
    return pl.pallas_call(
        attend_body,
        grid=(cols // step,),
        in_specs=[chunk(x), whole((1, width)), weight, weight, weight]
        + [whole(cos.shape), whole(sin.shape), whole((rows, rows))],
        out_specs=[whole((rows, width))] + [column] * 4,
        out_shape=[jax.ShapeDtypeStruct((rows, width), BF16)]
        + [jax.ShapeDtypeStruct((rows, cols), BF16)] * 4,
        cost_estimate=pl.CostEstimate(
            flops=6 * rows * width * cols + 16 * rows * rows * cols,
            bytes_accessed=4 * rows * width + 6 * width * cols + 8 * rows * cols,
            transcendentals=rows * rows * cols // HD,
        ),
    )(x, gain.reshape(1, width), wq, wk, wv, cos, sin, mask)


def attend_back_body(hidden, wo, q_in, k_in, v_in, attn_in, cos, sin, mask, *rest):
    out = rest[-1]
    grad = mm_nt(hidden[...], wo[...]).astype(BF16)
    allowed = mask[...]
    scale = HD ** (-0.5)
    q_all, k_all, v_all, attn = q_in[...], k_in[...], v_in[...], attn_in[...]
    q_list, k_list, v_list = [], [], []
    for h in range(grad.shape[1] // HD):
        at = slice(h * HD, (h + 1) * HD)
        q, k, v, g = q_all[:, at], k_all[:, at], v_all[:, at], grad[:, at]
        probs = head_probs(q, k, allowed)
        v_list.append(mm_tn(probs.astype(BF16), g))
        delta = jnp.sum(g.astype(F32) * attn[:, at].astype(F32), axis=-1, keepdims=True)
        score_grad = (probs * (mm_nt(g, v) - delta) * scale).astype(BF16)
        q_list.append(mm(score_grad, k))
        k_list.append(mm_tn(score_grad, q))
    cosine, back_sine = widen(cos[...], wo.shape[0]), -widen(sin[...], wo.shape[0])
    out[0] = turn(jnp.concatenate(q_list, axis=1), cosine, back_sine).astype(BF16)
    out[1] = turn(jnp.concatenate(k_list, axis=1), cosine, back_sine).astype(BF16)
    out[2] = jnp.concatenate(v_list, axis=1).astype(BF16)


def attend_back(hidden, wo, q, k, v, attn, cos, sin, mask, after):
    rows, width = hidden.shape
    cols = wo.shape[0]
    step = min(256, cols)
    column = pl.BlockSpec((rows, step), lambda i: (0, i))
    whole = lambda shape: pl.BlockSpec(shape, lambda i: (0, 0))
    return pl.pallas_call(
        attend_back_body,
        grid=(cols // step,),
        in_specs=[whole((rows, width)), pl.BlockSpec((step, width), lambda i: (i, 0))]
        + [column] * 4
        + [whole(cos.shape), whole(sin.shape), whole((rows, rows))]
        + [pl.BlockSpec(memory_space=pl.ANY)] * len(after),
        out_specs=pl.BlockSpec((3, rows, step), lambda i: (0, 0, i)),
        out_shape=jax.ShapeDtypeStruct((3, rows, cols), BF16),
        cost_estimate=pl.CostEstimate(
            flops=2 * rows * width * cols + 40 * rows * rows * cols,
            bytes_accessed=2 * rows * width + 2 * width * cols + 14 * rows * cols,
            transcendentals=rows * rows * cols // HD,
        ),
    )(hidden, wo, q, k, v, attn, cos, sin, mask, *after)


def flip_body(value, keep, out):
    kept = jnp.where(keep[...] > 0, value[...].astype(F32), 0.0)
    out[...] = kept.astype(BF16).T


def flip_rows(value, keep):
    rows, width = value.shape
    step = min(512, width)
    return pl.pallas_call(
        flip_body,
        grid=(width // step,),
        in_specs=[
            pl.BlockSpec((rows, step), lambda i: (0, i)),
            pl.BlockSpec((rows, 1), lambda i: (0, 0)),
        ],
        out_specs=pl.BlockSpec((step, rows), lambda i: (i, 0)),
        out_shape=jax.ShapeDtypeStruct((width, rows), BF16),
        cost_estimate=pl.CostEstimate(
            flops=rows * width, bytes_accessed=4 * rows * width, transcendentals=0
        ),
    )(value, keep.reshape(rows, 1))


def outer_body(shape, has_add, flipped, which, *refs):
    out, column, at = refs[-1], 0, 0
    adder = refs[-2] if has_add else None
    for count in shape:
        if flipped:
            rights = refs[at + 1 : at + 1 + count]
            lefts, start = [], 0
            for right in rights:
                lefts.append(refs[at][:, start : start + right.shape[0]])
                start += right.shape[0]
            at += 1 + count
        else:
            lefts = [refs[at + c][...].T for c in range(count)]
            rights = refs[at + count : at + 2 * count]
            at += 2 * count
        planes = rights[0].shape[0] if len(rights[0].shape) == 3 else 1
        width = rights[0].shape[-1]
        tile = min(512, width)
        for plane in range(planes):
            for start in range(0, width, tile):
                total = None
                for left, right in zip(lefts, rights):
                    span = pl.ds(start, tile)
                    block = right[plane, :, span] if len(right.shape) == 3 else right[:, span]
                    part = mm(left, block)
                    total = part if total is None else total + part
                span = pl.ds(column, tile)
                if has_add:
                    total = total + adder[:, span]
                out[:, span] = total
                column += tile


def outer(groups, which, pieces, add=None, part=(0, 1), flipped=False):
    piece = groups[0][0][0].shape[0 if flipped else 1] // pieces
    index, parts = part
    specs, args, out_cols, work, moved = [], [], 0, 0, 0
    for lefts, rights in groups:
        for v in lefts:
            if flipped:
                specs.append(pl.BlockSpec((piece, v.shape[1]), lambda j, w: (2 * j + w[0], 0)))
            else:
                specs.append(pl.BlockSpec((v.shape[0], piece), lambda j, w: (0, 2 * j + w[0])))
            moved += v.size
        for v in rights:
            if v.ndim == 3:
                cols = v.shape[0] * v.shape[2]
                specs.append(pl.BlockSpec(v.shape, lambda j, w: (0, 0, 0)))
            else:
                cols = v.shape[1] // parts
                specs.append(pl.BlockSpec((v.shape[0], cols), lambda j, w: (0, index)))
            moved += v.size // parts * 2
        work += sum(v.shape[-2] for v in rights) * cols
        out_cols += cols
        args += list(lefts) + list(rights)
    out_rows = pieces // 2 * piece
    out_spec = pl.BlockSpec((piece, out_cols), lambda j, w: (j, 0))
    if add is not None:
        specs.append(out_spec)
        args.append(add)
    return pl.pallas_call(
        functools.partial(outer_body, [len(g[1]) for g in groups], add is not None, flipped),
        grid_spec=pltpu.PrefetchScalarGridSpec(
            num_scalar_prefetch=1,
            grid=(pieces // 2,),
            in_specs=specs,
            out_specs=out_spec,
        ),
        out_shape=jax.ShapeDtypeStruct((out_rows, out_cols), F32),
        cost_estimate=pl.CostEstimate(
            flops=2 * work * out_rows,
            bytes_accessed=moved + 4 * out_rows * out_cols,
            transcendentals=0,
        ),
        name="outer",
    )(which.reshape(1).astype(jnp.int32), *args)


class Cube:
    def __init__(self, axis, size):
        self.axis = axis
        self.size = size
        self.bits = [1 << i for i in range(size.bit_length() - 1)]
        self.me = lax.axis_index(axis)

    def swap(self, value, bit):
        return lax.ppermute(value, self.axis, [(i, i ^ bit) for i in range(self.size)])

    def bit_of(self, bit):
        return (self.me >> (bit.bit_length() - 1)) & 1

    def own_start(self, rows, bits):
        start = 0
        for bit in bits:
            rows = rows // 2
            start = start + self.bit_of(bit) * rows
        return start

    def scatter(self, value, rows, bits):
        for bit in bits:
            half = rows // 2
            mine = self.bit_of(bit)
            away = lax.dynamic_slice_in_dim(value, (1 - mine) * half, half, 0)
            got = self.swap(away, bit)
            value = lax.dynamic_slice_in_dim(value, mine * half, half, 0) + got
            rows = half
        return value

    def gather(self, value, bits, after):
        for step, bit in enumerate(reversed(bits)):
            last = step == len(bits) - 1
            got = self.swap(value, bit)
            if last and after is not None:
                value, got, _ = lax.optimization_barrier((value, got, after))
            mine = self.bit_of(bit)
            value = jnp.where(
                mine == 0,
                jnp.concatenate([value, got], axis=0),
                jnp.concatenate([got, value], axis=0),
            )
        return value

    def total(self, value):
        for bit in self.bits:
            value = value + self.swap(value, bit)
        return value


def on_device(sizes):
    dp_size, tensor_size = sizes

    def run(
        block_input,
        block_owner,
        token_mask,
        attention_gain,
        query_weight,
        key_weight,
        value_weight,
        output_weight,
        feedforward_gain,
        gate_weight,
        up_weight,
        down_weight,
        cotangent,
    ):
        row_count, width = block_input.shape
        head_count = query_weight.shape[1] // HD
        head_cols = head_count * HD
        tensor = Cube(TP, tensor_size)
        data = Cube(DP, dp_size)
        core = data.bit_of(1)
        pair_lists = [[i for i in range(dp_size) if i % 2 == c] for c in range(2)]

        bounds = [(0, FIRST), (FIRST, row_count)]
        orders = (tensor.bits, tensor.bits[::-1])

        def halves(size):
            return [(0, size // 2, orders[0]), (size // 2, size // 2, orders[1])]

        def own_rows(value, low, size):
            return jnp.concatenate(
                [
                    lax.dynamic_slice_in_dim(
                        value, low + base + tensor.own_start(rows, bits), rows // tensor_size, 0
                    )
                    for base, rows, bits in halves(size)
                ],
                axis=0,
            )

        def scatter_rows(make, size):
            parts = halves(size)
            half = parts[0][1] // 2

            def piece(flip):
                starts = []
                for base, _, bits in parts:
                    mine = tensor.bit_of(bits[0])
                    starts.append(base + (1 - mine if flip else mine) * half)
                return make(starts, half)

            away = piece(True)
            got = [
                tensor.swap(away[i * half : (i + 1) * half], bits[0])
                for i, (_, _, bits) in enumerate(parts)
            ]
            keep = piece(False)
            return jnp.concatenate(
                [
                    tensor.scatter(keep[i * half : (i + 1) * half] + got[i], half, bits[1:])
                    for i, (_, _, bits) in enumerate(parts)
                ],
                axis=0,
            )

        def gather_rows(value, size, after=None):
            quarter = size // 2 // tensor_size
            return jnp.concatenate(
                [
                    tensor.gather(value[i * quarter : (i + 1) * quarter], bits, after)
                    for i, (_, _, bits) in enumerate(halves(size))
                ],
                axis=0,
            )

        def rows_of(value, starts, size):
            return jnp.concatenate(
                [lax.dynamic_slice_in_dim(value, start, size, 0) for start in starts], axis=0
            )

        def core_sum(groups, part=(0, 1), flipped=False):
            away = outer(groups, 1 - core, dp_size, part=part, flipped=flipped)
            got = data.swap(away, 1)
            return outer(groups, core, dp_size, add=got, part=part, flipped=flipped)

        def z_scatter(value):
            return lax.psum_scatter(
                value, DP, scatter_dimension=0, tiled=True, axis_index_groups=pair_lists
            )

        first_block = lax.axis_index(DP) * (row_count // BLK)
        owners = jnp.broadcast_to(block_owner[:, None], (row_count // BLK, BLK)).reshape(-1)
        row_index = jnp.arange(row_count, dtype=jnp.int32)
        positions = (row_index // BLK + first_block - owners) * BLK + row_index % BLK
        saved = []
        for lo, hi in bounds:
            size = hi - lo
            x_f = block_input[lo:hi].astype(F32)
            rows = jnp.where(
                token_mask[lo:hi, None] > 0, cotangent[lo:hi], jnp.zeros_like(cotangent[lo:hi])
            )
            aligned = lo % size == 0
            cut = (lambda v: v) if aligned else (lambda v, lo=lo, hi=hi: v[lo:hi])
            row_block = lo // size if aligned else 0
            own_g, pos_g, mask_g = owners[lo:hi], positions[lo:hi], token_mask[lo:hi]
            if saved:
                own_g, pos_g, mask_g, _ = lax.optimization_barrier(
                    (own_g, pos_g, mask_g, saved[-1].flat)
                )
            cos_g, sin_g = rope_tables(pos_g, min(128, head_cols))
            allowed = (
                (own_g[:, None] == own_g[None, :])
                & (pos_g[None, :] <= pos_g[:, None])
                & ((mask_g[None, :] > 0) | (pos_g[None, :] == 0))
            ).astype(F32)
            act, q, k, v, flat = attend(
                cut(block_input), row_block, attention_gain, query_weight, key_weight, value_weight,
                cos_g, sin_g, allowed,
            )
            added = scatter_rows(
                lambda s, n, flat=flat: mm(rows_of(flat, s, n), output_weight), size
            )
            x_own = own_rows(block_input, lo, size).astype(F32)
            hid = x_own + added
            inv_two = lax.rsqrt(jnp.mean(hid * hid, axis=-1, keepdims=True) + NORM_EPS)
            after = saved[-1].act_two if saved else None
            unit = gather_rows(hid * inv_two, size, after)
            act_two = (unit * feedforward_gain).astype(BF16)
            saved.append(
                SimpleNamespace(q=q, k=k, v=v, allowed=allowed, flat=flat, act=act, rows=rows, x_f=x_f,
                     cos=cos_g, sin=sin_g, x_own=x_own, hid=hid, added=added, inv_two=inv_two,
                     act_two=act_two)
            )

        for s in saved:
            s.inner_grad = mm_nt(s.rows, down_weight)
            s.gate_pre = mm(s.act_two, gate_weight)
            s.up_pre = mm(s.act_two, up_weight)
            s.sig = jax.nn.sigmoid(s.gate_pre)
            s.inner = (s.gate_pre * s.sig * s.up_pre).astype(BF16)
        flipped_rows = flip_rows(cotangent, token_mask)
        down_parts = [
            core_sum([([flipped_rows], [s.inner for s in saved])], (i, 2), True)
            for i in range(2)
        ]
        down_sums = [z_scatter(v) for v in down_parts]

        gain_parts = jnp.zeros((width,), F32)
        for index, ((lo, hi), s) in enumerate(zip(bounds, saved)):
            size = hi - lo
            rows = s.rows
            inner_grad = s.inner_grad
            gate_pre, up_pre, sig = s.gate_pre, s.up_pre, s.sig
            if index:
                gate_pre, up_pre, _ = lax.optimization_barrier((gate_pre, up_pre, down_parts))
            gate_back = (inner_grad * up_pre * sig * (1.0 + gate_pre * (1.0 - sig))).astype(BF16)
            up_back = (inner_grad * gate_pre * sig).astype(BF16)
            s.gate_back, s.up_back = gate_back, up_back
            part = scatter_rows(
                lambda st, n, a=gate_back, b=up_back: mm_nt(rows_of(a, st, n), gate_weight)
                + mm_nt(rows_of(b, st, n), up_weight),
                size,
            )
            s.part = part
            unit = s.hid * s.inv_two
            gain_parts = gain_parts + jnp.sum(part * unit, axis=0)
            scaled = part * feedforward_gain
            back = s.inv_two * (
                scaled - unit * jnp.mean(scaled * unit, axis=-1, keepdims=True)
            )
            s.hidden_grad = own_rows(rows, 0, size).astype(F32) + back
            after = saved[index - 1].hidden_back if index else None
            full = gather_rows(back, size, after)
            s.hidden_back = (rows.astype(F32) + full).astype(BF16)

        both_part = core_sum(
            [([s.act_two for s in saved], [s.gate_back for s in saved]), ([s.act_two for s in saved], [s.up_back for s in saved])],
        )
        both_sum = z_scatter(both_part)

        outs = []
        for s in saved:
            size = s.rows.shape[0]
            late_inner, _ = lax.optimization_barrier((s.inner, saved[-1].part))
            mlp = scatter_rows(lambda st, n, a=late_inner: mm(rows_of(a, st, n), down_weight), size)
            full = gather_rows(s.added + mlp, size)
            outs.append((s.x_f + full).astype(BF16))
        block_output = jnp.concatenate(outs, axis=0)

        first_parts = jnp.zeros((width,), F32)
        input_grads = []
        for (lo, hi), s in zip(bounds, saved):
            size = hi - lo
            back3 = attend_back(
                s.hidden_back, output_weight, s.q, s.k, s.v, s.flat,
                s.cos, s.sin, s.allowed, (both_part,),
            )
            s.qkv_back = back3
            q_back, k_back, v_back = back3[0], back3[1], back3[2]
            part = scatter_rows(
                lambda st, n, a=q_back, b=k_back, c=v_back: mm_nt(rows_of(a, st, n), query_weight)
                + mm_nt(rows_of(b, st, n), key_weight)
                + mm_nt(rows_of(c, st, n), value_weight),
                size,
            )
            x_own = s.x_own
            inv_one = lax.rsqrt(jnp.mean(x_own * x_own, axis=-1, keepdims=True) + NORM_EPS)
            unit = x_own * inv_one
            first_parts = first_parts + jnp.sum(part * unit, axis=0)
            scaled = part * attention_gain
            back = inv_one * (scaled - unit * jnp.mean(scaled * unit, axis=-1, keepdims=True))
            input_grads.append(gather_rows(s.hidden_grad + back, size))
        input_gradient = jnp.concatenate(input_grads, axis=0)

        last_part = core_sum(
            [([s.act for s in saved], [s.qkv_back for s in saved]), ([s.hidden_back for s in saved], [s.flat for s in saved])]
        )
        last_sum = z_scatter(last_part)
        down_sums, both_sum, _ = lax.optimization_barrier((down_sums, both_sum, last_part))
        down_sum = jnp.concatenate([v.T for v in down_sums], axis=0)
        ff_cols = gate_weight.shape[1]
        gate_sum, up_sum = both_sum[:, :ff_cols], both_sum[:, ff_cols:]
        query_sum = last_sum[:, :head_cols]
        key_sum = last_sum[:, head_cols : 2 * head_cols]
        value_sum = last_sum[:, 2 * head_cols : 3 * head_cols]
        out_sum = last_sum[:, 3 * head_cols :].T

        gains = data.total(tensor.total(jnp.stack([first_parts, gain_parts])))
        gain_piece = width // dp_size
        gains = lax.dynamic_slice_in_dim(gains, lax.axis_index(DP) * gain_piece, gain_piece, 1)
        return (
            block_output,
            input_gradient,
            gains[0],
            query_sum,
            key_sum,
            value_sum,
            out_sum,
            gains[1],
            gate_sum,
            up_sum,
            down_sum,
        )

    return run


def solution(mesh):
    sizes = (mesh.shape[DP], mesh.shape[TP])
    body = on_device(sizes)

    return jax.shard_map(
        body,
        mesh=mesh,
        in_specs=(
            P(DP, None),
            P(DP),
            P(DP),
            P(),
            P(None, TP),
            P(None, TP),
            P(None, TP),
            P(TP, None),
            P(),
            P(None, TP),
            P(None, TP),
            P(TP, None),
            P(DP, None),
        ),
        out_specs=(
            P(DP, None),
            P(DP, None),
            P(DP),
            P(DP, TP),
            P(DP, TP),
            P(DP, TP),
            P(TP, DP),
            P(DP),
            P(DP, TP),
            P(DP, TP),
            P(TP, DP),
        ),
        check_vma=False,
    )
```

```python
import functools
from types import SimpleNamespace

import jax
import jax.numpy as jnp
from jax import lax
from jax.experimental import pallas as pl
from jax.experimental.pallas import tpu as pltpu
from jax.sharding import PartitionSpec as P


HD = 64
BLK = 128
SEQ_BLOCKS = 4
FIRST = BLK * SEQ_BLOCKS

NORM_EPS = 1e-05
ROPE_BASE = 130000.0
MASKED = -1e30


DP, TP = "dp", "tensor"

F32 = jnp.float32
BF16 = jnp.bfloat16


def mm(a, b):
    return jnp.dot(a, b, preferred_element_type=F32)


def mm_nt(a, b):
    return lax.dot_general(a, b, (((1,), (1,)), ((), ())), preferred_element_type=F32)


def mm_tn(a, b):
    return lax.dot_general(a, b, (((0,), (0,)), ((), ())), preferred_element_type=F32)


def rope_tables(positions, lanes):
    half_width = HD // 2
    lane = jnp.arange(lanes, dtype=jnp.int32)
    frequency = ROPE_BASE ** (-((lane % half_width).astype(F32) * 2.0 / HD))
    sign = jnp.where(lane % HD < half_width, -1.0, 1.0).astype(F32)
    angles = positions.astype(F32)[:, None] * frequency[None, :]
    return jnp.cos(angles), jnp.sin(angles) * sign[None, :]


def widen(table, lanes):
    return jnp.concatenate([table] * (lanes // table.shape[1]), axis=1)


def turn(values, cosine, signed_sine):
    lanes = values.shape[1]
    half = HD // 2
    lane = lax.broadcasted_iota(jnp.int32, values.shape, 1)
    other = jnp.where(
        lane % HD < half,
        pltpu.roll(values, lanes - half, 1),
        pltpu.roll(values, half, 1),
    )
    return values * cosine + other * signed_sine


def head_probs(q, k, mask):
    scores = mm_nt(q, k) * HD ** (-0.5)
    scores = jnp.where(mask > 0, scores, MASKED)
    peak = jnp.max(scores, axis=-1, keepdims=True)
    raised = jnp.exp(scores - peak)
    return raised * (1.0 / jnp.sum(raised, axis=-1, keepdims=True))


def attend_body(x, gain, wq, wk, wv, cos, sin, mask, act_out, q_out, k_out, v_out, attn_out):
    @pl.when(pl.program_id(0) == 0)
    def _():
        values = x[...].astype(F32)
        inverse = lax.rsqrt(jnp.mean(values * values, axis=-1, keepdims=True) + NORM_EPS)
        act_out[...] = (values * inverse * gain[...]).astype(BF16)

    rows = act_out[...]
    cosine = widen(cos[...], wq.shape[1])
    sine = widen(sin[...], wq.shape[1])
    q = turn(mm(rows, wq[...]), cosine, sine).astype(BF16)
    k = turn(mm(rows, wk[...]), cosine, sine).astype(BF16)
    v = mm(rows, wv[...]).astype(BF16)
    q_out[...] = q
    k_out[...] = k
    v_out[...] = v
    count = rows.shape[0]
    tile = min(256, count)
    for start in range(0, count, tile):
        end = start + tile
        allowed = mask[start:end, :end]
        outs = []
        for h in range(q.shape[1] // HD):
            at = slice(h * HD, (h + 1) * HD)
            probs = head_probs(q[start:end, at], k[:end, at], allowed)
            outs.append(mm(probs.astype(BF16), v[:end, at]))
        attn_out[start:end, :] = jnp.concatenate(outs, axis=1).astype(BF16)


def attend(x, row_block, gain, wq, wk, wv, cos, sin, mask):
    rows, width = mask.shape[0], x.shape[1]
    cols = wq.shape[1]
    step = min(256, cols)
    column = pl.BlockSpec((rows, step), lambda i: (0, i))
    whole = lambda shape: pl.BlockSpec(shape, lambda i: (0, 0))
    chunk = lambda v: pl.BlockSpec((rows, v.shape[1]), lambda i: (row_block, 0))
    weight = pl.BlockSpec((width, step), lambda i: (0, i))
    return pl.pallas_call(
        attend_body,
        grid=(cols // step,),
        in_specs=[chunk(x), whole((1, width)), weight, weight, weight]
        + [whole(cos.shape), whole(sin.shape), whole((rows, rows))],
        out_specs=[whole((rows, width))] + [column] * 4,
        out_shape=[jax.ShapeDtypeStruct((rows, width), BF16)]
        + [jax.ShapeDtypeStruct((rows, cols), BF16)] * 4,
        cost_estimate=pl.CostEstimate(
            flops=6 * rows * width * cols + 16 * rows * rows * cols,
            bytes_accessed=4 * rows * width + 6 * width * cols + 8 * rows * cols,
            transcendentals=rows * rows * cols // HD,
        ),
    )(x, gain.reshape(1, width), wq, wk, wv, cos, sin, mask)


def attend_back_body(hidden, wo, q_in, k_in, v_in, attn_in, cos, sin, mask, *rest):
    out = rest[-1]
    grad = mm_nt(hidden[...], wo[...]).astype(BF16)
    allowed = mask[...]
    scale = HD ** (-0.5)
    q_all, k_all, v_all, attn = q_in[...], k_in[...], v_in[...], attn_in[...]
    q_list, k_list, v_list = [], [], []
    for h in range(grad.shape[1] // HD):
        at = slice(h * HD, (h + 1) * HD)
        q, k, v, g = q_all[:, at], k_all[:, at], v_all[:, at], grad[:, at]
        probs = head_probs(q, k, allowed)
        v_list.append(mm_tn(probs.astype(BF16), g))
        delta = jnp.sum(g.astype(F32) * attn[:, at].astype(F32), axis=-1, keepdims=True)
        score_grad = (probs * (mm_nt(g, v) - delta) * scale).astype(BF16)
        q_list.append(mm(score_grad, k))
        k_list.append(mm_tn(score_grad, q))
    cosine, back_sine = widen(cos[...], wo.shape[0]), -widen(sin[...], wo.shape[0])
    out[0] = turn(jnp.concatenate(q_list, axis=1), cosine, back_sine).astype(BF16)
    out[1] = turn(jnp.concatenate(k_list, axis=1), cosine, back_sine).astype(BF16)
    out[2] = jnp.concatenate(v_list, axis=1).astype(BF16)


def attend_back(hidden, wo, q, k, v, attn, cos, sin, mask, after):
    rows, width = hidden.shape
    cols = wo.shape[0]
    step = min(256, cols)
    column = pl.BlockSpec((rows, step), lambda i: (0, i))
    whole = lambda shape: pl.BlockSpec(shape, lambda i: (0, 0))
    return pl.pallas_call(
        attend_back_body,
        grid=(cols // step,),
        in_specs=[whole((rows, width)), pl.BlockSpec((step, width), lambda i: (i, 0))]
        + [column] * 4
        + [whole(cos.shape), whole(sin.shape), whole((rows, rows))]
        + [pl.BlockSpec(memory_space=pl.ANY)] * len(after),
        out_specs=pl.BlockSpec((3, rows, step), lambda i: (0, 0, i)),
        out_shape=jax.ShapeDtypeStruct((3, rows, cols), BF16),
        cost_estimate=pl.CostEstimate(
            flops=2 * rows * width * cols + 40 * rows * rows * cols,
            bytes_accessed=2 * rows * width + 2 * width * cols + 14 * rows * cols,
            transcendentals=rows * rows * cols // HD,
        ),
    )(hidden, wo, q, k, v, attn, cos, sin, mask, *after)


def flip_body(value, keep, out):
    kept = jnp.where(keep[...] > 0, value[...].astype(F32), 0.0)
    out[...] = kept.astype(BF16).T


def flip_rows(value, keep):
    rows, width = value.shape
    step = min(512, width)
    return pl.pallas_call(
        flip_body,
        grid=(width // step,),
        in_specs=[
            pl.BlockSpec((rows, step), lambda i: (0, i)),
            pl.BlockSpec((rows, 1), lambda i: (0, 0)),
        ],
        out_specs=pl.BlockSpec((step, rows), lambda i: (i, 0)),
        out_shape=jax.ShapeDtypeStruct((width, rows), BF16),
        cost_estimate=pl.CostEstimate(
            flops=rows * width, bytes_accessed=4 * rows * width, transcendentals=0
        ),
    )(value, keep.reshape(rows, 1))


def outer_body(shape, has_add, flipped, which, *refs):
    out, column, at = refs[-1], 0, 0
    adder = refs[-2] if has_add else None
    for count in shape:
        if flipped:
            rights = refs[at + 1 : at + 1 + count]
            lefts, start = [], 0
            for right in rights:
                lefts.append(refs[at][:, start : start + right.shape[0]])
                start += right.shape[0]
            at += 1 + count
        else:
            lefts = [refs[at + c][...].T for c in range(count)]
            rights = refs[at + count : at + 2 * count]
            at += 2 * count
        planes = rights[0].shape[0] if len(rights[0].shape) == 3 else 1
        width = rights[0].shape[-1]
        tile = min(512, width)
        for plane in range(planes):
            for start in range(0, width, tile):
                total = None
                for left, right in zip(lefts, rights):
                    span = pl.ds(start, tile)
                    block = right[plane, :, span] if len(right.shape) == 3 else right[:, span]
                    part = mm(left, block)
                    total = part if total is None else total + part
                span = pl.ds(column, tile)
                if has_add:
                    total = total + adder[:, span]
                out[:, span] = total
                column += tile


def outer(groups, which, pieces, add=None, part=None, flipped=False):
    piece = groups[0][0][0].shape[0 if flipped else 1] // pieces
    indices, parts = part or ((0,) * len(groups), 1)
    specs, args, out_cols, work, moved = [], [], 0, 0, 0
    for index, (lefts, rights) in zip(indices, groups):
        for v in lefts:
            if flipped:
                specs.append(pl.BlockSpec((piece, v.shape[1]), lambda j, w: (2 * j + w[0], 0)))
            else:
                specs.append(pl.BlockSpec((v.shape[0], piece), lambda j, w: (0, 2 * j + w[0])))
            moved += v.size
        for v in rights:
            if v.ndim == 3:
                cols = v.shape[0] * v.shape[2]
                specs.append(pl.BlockSpec(v.shape, lambda j, w: (0, 0, 0)))
            else:
                cols = v.shape[1] // parts
                specs.append(pl.BlockSpec((v.shape[0], cols), lambda j, w, at=index: (0, at)))
            moved += v.size // parts * 2
        work += sum(v.shape[-2] for v in rights) * cols
        out_cols += cols
        args += list(lefts) + list(rights)
    out_rows = pieces // 2 * piece
    out_spec = pl.BlockSpec((piece, out_cols), lambda j, w: (j, 0))
    if add is not None:
        specs.append(out_spec)
        args.append(add)
    return pl.pallas_call(
        functools.partial(outer_body, [len(g[1]) for g in groups], add is not None, flipped),
        grid_spec=pltpu.PrefetchScalarGridSpec(
            num_scalar_prefetch=1,
            grid=(pieces // 2,),
            in_specs=specs,
            out_specs=out_spec,
        ),
        out_shape=jax.ShapeDtypeStruct((out_rows, out_cols), F32),
        cost_estimate=pl.CostEstimate(
            flops=2 * work * out_rows,
            bytes_accessed=moved + 4 * out_rows * out_cols,
            transcendentals=0,
        ),
        name="outer",
    )(which.reshape(1).astype(jnp.int32), *args)


class Cube:
    def __init__(self, axis, size):
        self.axis = axis
        self.size = size
        self.bits = [1 << i for i in range(size.bit_length() - 1)]
        self.me = lax.axis_index(axis)

    def swap(self, value, bit):
        return lax.ppermute(value, self.axis, [(i, i ^ bit) for i in range(self.size)])

    def bit_of(self, bit):
        return (self.me >> (bit.bit_length() - 1)) & 1

    def own_start(self, rows, bits):
        start = 0
        for bit in bits:
            rows = rows // 2
            start = start + self.bit_of(bit) * rows
        return start

    def scatter(self, value, rows, bits):
        for bit in bits:
            half = rows // 2
            mine = self.bit_of(bit)
            away = lax.dynamic_slice_in_dim(value, (1 - mine) * half, half, 0)
            got = self.swap(away, bit)
            value = lax.dynamic_slice_in_dim(value, mine * half, half, 0) + got
            rows = half
        return value

    def gather(self, value, bits, after):
        for step, bit in enumerate(reversed(bits)):
            last = step == len(bits) - 1
            got = self.swap(value, bit)
            if last and after is not None:
                value, got, _ = lax.optimization_barrier((value, got, after))
            mine = self.bit_of(bit)
            value = jnp.where(
                mine == 0,
                jnp.concatenate([value, got], axis=0),
                jnp.concatenate([got, value], axis=0),
            )
        return value

    def total(self, value):
        for bit in self.bits:
            value = value + self.swap(value, bit)
        return value


def on_device(sizes):
    dp_size, tensor_size = sizes

    def run(
        block_input,
        block_owner,
        token_mask,
        attention_gain,
        query_weight,
        key_weight,
        value_weight,
        output_weight,
        feedforward_gain,
        gate_weight,
        up_weight,
        down_weight,
        cotangent,
    ):
        row_count, width = block_input.shape
        head_count = query_weight.shape[1] // HD
        head_cols = head_count * HD
        tensor = Cube(TP, tensor_size)
        data = Cube(DP, dp_size)
        core = data.bit_of(1)
        pair_lists = [[i for i in range(dp_size) if i % 2 == c] for c in range(2)]

        bounds = [(0, FIRST), (FIRST, row_count)]
        orders = (tensor.bits, tensor.bits[::-1])

        def halves(size):
            return [(0, size // 2, orders[0]), (size // 2, size // 2, orders[1])]

        def own_rows(value, low, size):
            return jnp.concatenate(
                [
                    lax.dynamic_slice_in_dim(
                        value, low + base + tensor.own_start(rows, bits), rows // tensor_size, 0
                    )
                    for base, rows, bits in halves(size)
                ],
                axis=0,
            )

        def scatter_rows(make, size):
            parts = halves(size)
            half = parts[0][1] // 2

            def piece(flip):
                starts = []
                for base, _, bits in parts:
                    mine = tensor.bit_of(bits[0])
                    starts.append(base + (1 - mine if flip else mine) * half)
                return make(starts, half)

            away = piece(True)
            got = [
                tensor.swap(away[i * half : (i + 1) * half], bits[0])
                for i, (_, _, bits) in enumerate(parts)
            ]
            keep = piece(False)
            return jnp.concatenate(
                [
                    tensor.scatter(keep[i * half : (i + 1) * half] + got[i], half, bits[1:])
                    for i, (_, _, bits) in enumerate(parts)
                ],
                axis=0,
            )

        def gather_rows(value, size, after=None):
            quarter = size // 2 // tensor_size
            return jnp.concatenate(
                [
                    tensor.gather(value[i * quarter : (i + 1) * quarter], bits, after)
                    for i, (_, _, bits) in enumerate(halves(size))
                ],
                axis=0,
            )

        def rows_of(value, starts, size):
            return jnp.concatenate(
                [lax.dynamic_slice_in_dim(value, start, size, 0) for start in starts], axis=0
            )

        def core_sum(groups, part=None, flipped=False):
            away = outer(groups, 1 - core, dp_size, part=part, flipped=flipped)
            got = data.swap(away, 1)
            return outer(groups, core, dp_size, add=got, part=part, flipped=flipped)

        def z_scatter(value):
            return lax.psum_scatter(
                value, DP, scatter_dimension=0, tiled=True, axis_index_groups=pair_lists
            )

        first_block = lax.axis_index(DP) * (row_count // BLK)
        owners = jnp.broadcast_to(block_owner[:, None], (row_count // BLK, BLK)).reshape(-1)
        row_index = jnp.arange(row_count, dtype=jnp.int32)
        positions = (row_index // BLK + first_block - owners) * BLK + row_index % BLK
        saved = []
        for lo, hi in bounds:
            size = hi - lo
            x_f = block_input[lo:hi].astype(F32)
            rows = jnp.where(
                token_mask[lo:hi, None] > 0, cotangent[lo:hi], jnp.zeros_like(cotangent[lo:hi])
            )
            aligned = lo % size == 0
            cut = (lambda v: v) if aligned else (lambda v, lo=lo, hi=hi: v[lo:hi])
            row_block = lo // size if aligned else 0
            own_g, pos_g, mask_g = owners[lo:hi], positions[lo:hi], token_mask[lo:hi]
            if saved:
                own_g, pos_g, mask_g, _ = lax.optimization_barrier(
                    (own_g, pos_g, mask_g, saved[-1].flat)
                )
            cos_g, sin_g = rope_tables(pos_g, min(128, head_cols))
            allowed = (
                (own_g[:, None] == own_g[None, :])
                & (pos_g[None, :] <= pos_g[:, None])
                & ((mask_g[None, :] > 0) | (pos_g[None, :] == 0))
            ).astype(F32)
            act, q, k, v, flat = attend(
                cut(block_input), row_block, attention_gain, query_weight, key_weight, value_weight,
                cos_g, sin_g, allowed,
            )
            added = scatter_rows(
                lambda s, n, flat=flat: mm(rows_of(flat, s, n), output_weight), size
            )
            x_own = own_rows(block_input, lo, size).astype(F32)
            hid = x_own + added
            inv_two = lax.rsqrt(jnp.mean(hid * hid, axis=-1, keepdims=True) + NORM_EPS)
            after = saved[-1].act_two if saved else None
            unit = gather_rows(hid * inv_two, size, after)
            act_two = (unit * feedforward_gain).astype(BF16)
            saved.append(
                SimpleNamespace(q=q, k=k, v=v, allowed=allowed, flat=flat, act=act, rows=rows, x_f=x_f,
                     cos=cos_g, sin=sin_g, x_own=x_own, hid=hid, added=added, inv_two=inv_two,
                     act_two=act_two)
            )

        for s in saved:
            s.inner_grad = mm_nt(s.rows, down_weight)
            s.gate_pre = mm(s.act_two, gate_weight)
            s.up_pre = mm(s.act_two, up_weight)
            s.sig = jax.nn.sigmoid(s.gate_pre)
            s.inner = (s.gate_pre * s.sig * s.up_pre).astype(BF16)
        flipped_rows = flip_rows(cotangent, token_mask)
        down_parts = [
            core_sum([([flipped_rows], [s.inner for s in saved])] * len(at), (at, 4), True)
            for at in ((0,), (1, 2, 3))
        ]
        down_sums = [z_scatter(v) for v in down_parts]

        gain_parts = jnp.zeros((width,), F32)
        for index, ((lo, hi), s) in enumerate(zip(bounds, saved)):
            size = hi - lo
            rows = s.rows
            inner_grad = s.inner_grad
            gate_pre, up_pre, sig = s.gate_pre, s.up_pre, s.sig
            if index:
                gate_pre, up_pre, _ = lax.optimization_barrier((gate_pre, up_pre, down_parts))
            gate_back = (inner_grad * up_pre * sig * (1.0 + gate_pre * (1.0 - sig))).astype(BF16)
            up_back = (inner_grad * gate_pre * sig).astype(BF16)
            s.gate_back, s.up_back = gate_back, up_back
            part = scatter_rows(
                lambda st, n, a=gate_back, b=up_back: mm_nt(rows_of(a, st, n), gate_weight)
                + mm_nt(rows_of(b, st, n), up_weight),
                size,
            )
            s.part = part
            unit = s.hid * s.inv_two
            gain_parts = gain_parts + jnp.sum(part * unit, axis=0)
            scaled = part * feedforward_gain
            back = s.inv_two * (
                scaled - unit * jnp.mean(scaled * unit, axis=-1, keepdims=True)
            )
            s.hidden_grad = own_rows(rows, 0, size).astype(F32) + back
            after = saved[index - 1].hidden_back if index else None
            full = gather_rows(back, size, after)
            s.hidden_back = (rows.astype(F32) + full).astype(BF16)

        both_part = core_sum(
            [([s.act_two for s in saved], [s.gate_back for s in saved]), ([s.act_two for s in saved], [s.up_back for s in saved])],
        )
        both_sum = z_scatter(both_part)

        outs = []
        for s in saved:
            size = s.rows.shape[0]
            late_inner, _ = lax.optimization_barrier((s.inner, saved[-1].part))
            mlp = scatter_rows(lambda st, n, a=late_inner: mm(rows_of(a, st, n), down_weight), size)
            full = gather_rows(s.added + mlp, size)
            outs.append((s.x_f + full).astype(BF16))
        block_output = jnp.concatenate(outs, axis=0)

        first_parts = jnp.zeros((width,), F32)
        input_grads = []
        for (lo, hi), s in zip(bounds, saved):
            size = hi - lo
            back3 = attend_back(
                s.hidden_back, output_weight, s.q, s.k, s.v, s.flat,
                s.cos, s.sin, s.allowed, (both_part,),
            )
            s.qkv_back = back3
            q_back, k_back, v_back = back3[0], back3[1], back3[2]
            part = scatter_rows(
                lambda st, n, a=q_back, b=k_back, c=v_back: mm_nt(rows_of(a, st, n), query_weight)
                + mm_nt(rows_of(b, st, n), key_weight)
                + mm_nt(rows_of(c, st, n), value_weight),
                size,
            )
            x_own = s.x_own
            inv_one = lax.rsqrt(jnp.mean(x_own * x_own, axis=-1, keepdims=True) + NORM_EPS)
            unit = x_own * inv_one
            first_parts = first_parts + jnp.sum(part * unit, axis=0)
            scaled = part * attention_gain
            back = inv_one * (scaled - unit * jnp.mean(scaled * unit, axis=-1, keepdims=True))
            input_grads.append(gather_rows(s.hidden_grad + back, size))
        input_gradient = jnp.concatenate(input_grads, axis=0)

        last_part = core_sum(
            [([s.act for s in saved], [s.qkv_back for s in saved]), ([s.hidden_back for s in saved], [s.flat for s in saved])]
        )
        last_sum = z_scatter(last_part)
        down_sums, both_sum, _ = lax.optimization_barrier((down_sums, both_sum, last_part))
        down_sum = jnp.concatenate([v.T for v in down_sums], axis=0)
        ff_cols = gate_weight.shape[1]
        gate_sum, up_sum = both_sum[:, :ff_cols], both_sum[:, ff_cols:]
        query_sum = last_sum[:, :head_cols]
        key_sum = last_sum[:, head_cols : 2 * head_cols]
        value_sum = last_sum[:, 2 * head_cols : 3 * head_cols]
        out_sum = last_sum[:, 3 * head_cols :].T

        gains = data.total(tensor.total(jnp.stack([first_parts, gain_parts])))
        gain_piece = width // dp_size
        gains = lax.dynamic_slice_in_dim(gains, lax.axis_index(DP) * gain_piece, gain_piece, 1)
        return (
            block_output,
            input_gradient,
            gains[0],
            query_sum,
            key_sum,
            value_sum,
            out_sum,
            gains[1],
            gate_sum,
            up_sum,
            down_sum,
        )

    return run


def solution(mesh):
    sizes = (mesh.shape[DP], mesh.shape[TP])
    body = on_device(sizes)

    return jax.shard_map(
        body,
        mesh=mesh,
        in_specs=(
            P(DP, None),
            P(DP),
            P(DP),
            P(),
            P(None, TP),
            P(None, TP),
            P(None, TP),
            P(TP, None),
            P(),
            P(None, TP),
            P(None, TP),
            P(TP, None),
            P(DP, None),
        ),
        out_specs=(
            P(DP, None),
            P(DP, None),
            P(DP),
            P(DP, TP),
            P(DP, TP),
            P(DP, TP),
            P(TP, DP),
            P(DP),
            P(DP, TP),
            P(DP, TP),
            P(TP, DP),
        ),
        check_vma=False,
    )
```
